32 devices in a mesh: groups: 2 (over y), ctx: 16 (over z, x, core).
Axes of the slice: x: 2, y: 2, z: 4, core: 2. Of those that a mesh axis runs over, the one named last changes fastest.
Arguments:
- normed_input: bfloat16 [2048, 8192], P(('groups', 'ctx')), parts along dimension 0, may hold values from -5 to 5
- query_base: bfloat16 [2048, 4096], P(('groups', 'ctx')), parts along dimension 0, may hold values from -6 to 6
- key_base: bfloat16 [2048, 512], P(('groups', 'ctx')), parts along dimension 0, may hold values from -6 to 6
- value_base: bfloat16 [2048, 512], P(('groups', 'ctx')), parts along dimension 0, may hold values from -4 to 4
- adapter_pool: bfloat16 [16, 2686976], P('ctx'), may hold values from -1 to 1
- stretch_adapter: int32 [4], P('groups'), parts along dimension 0, may hold values from 0 to 15
- adapter_owner: int32 [16], replicated, may hold values from 0 to 15, each once
Outputs:
- attended: bfloat16 [2048, 4096], P(('groups', 'ctx')), parts along dimension 0
- out_delta: bfloat16 [2048, 8192], P(('groups', 'ctx')), parts along dimension 0
The draws below stay inside these ranges and needn't reach their ends.
There are 2 independent parts, one for each index of `groups`. The reference program is written for one: setup_inputs(seed, part) draws one part's arguments, and reference() takes and returns one part's arrays. A program takes and returns all parts, laid end to end along the dimension named above; an argument that names none is the same for every part. Nothing has to cross between parts.
All inputs are finite; a program needn't handle non-finite values.
Results may differ from the reference program's by a relative error of at most 0.018.
Values may be sent and summed in bfloat16 or wider, within the bound.
A program may use at most 192 MiB of HBM per device.

```python
import math
import jax
import jax.numpy as jnp
import numpy as np
from jax import lax

D = 8192
QH = 32
KEYVALUE_HEADS = 4
HEAD_SIZE = 128
ADAPTER_RANK = 64
BLOCK_TOKENS = 512
SEQ = 1024
NCHUNK = 2
ADAPTERS = 16
QKV_POOL = 1900544
POOL = 2686976


def draw_query_base(key, part):
    return jnp.clip(jax.random.normal(jax.random.fold_in(key, 11), (SEQ, QH * HEAD_SIZE), jnp.float32), -4.0, 4.0).astype(jnp.bfloat16)


def draw_key_base(key, part):
    return jnp.clip(jax.random.normal(jax.random.fold_in(key, 13), (SEQ, KEYVALUE_HEADS * HEAD_SIZE), jnp.float32), -4.0, 4.0).astype(jnp.bfloat16)


def draw_adapter_pool(key, part):
    raw_values = jnp.clip(jax.random.normal(jax.random.fold_in(key, 17), (ADAPTERS, POOL), jnp.float32), -4.0, 4.0)
    column = jnp.arange(POOL)
    bound_one = 3 * ADAPTER_RANK * D
    bound_two = bound_one + ADAPTER_RANK * QH * HEAD_SIZE
    bound_three = bound_two + 2 * ADAPTER_RANK * KEYVALUE_HEADS * HEAD_SIZE
    bound_four = bound_three + ADAPTER_RANK * QH * HEAD_SIZE
    in_keyval = (column - bound_two) % (2 * KEYVALUE_HEADS * HEAD_SIZE)
    column_scale = jnp.where(column < bound_one, D ** (-0.5), jnp.where(column < bound_two, 0.01, jnp.where(column < bound_three, jnp.where(in_keyval < KEYVALUE_HEADS * HEAD_SIZE, 0.01, 0.06), jnp.where(column < bound_four, (QH * HEAD_SIZE) ** (-0.5), 0.25))))
    return (raw_values * column_scale.astype(jnp.float32)[None, :]).astype(jnp.bfloat16)


def block_levels(stream_key, extent, split, low, top_value):
    gain = 1.0
    for dim, parts in split:
        draws = jax.random.uniform(jax.random.fold_in(jax.random.fold_in(stream_key, 6), dim), (parts,), jnp.float32, low / len(split), top_value / len(split))
        gain = gain * jnp.repeat(jnp.exp(draws), extent[dim] // parts).reshape((-1,) + (1,) * (len(extent) - 1 - dim))
    return gain


def rank_bounds(amount, lean):
    portions = [(1 << 20) // math.isqrt(standing ** lean) + 1 for standing in range(1, amount + 1)]
    spread = 1 + sum(portions) // (1 << 30)
    return np.cumsum(np.array([max(1, weight // spread) for weight in portions]))


def ranked(stream_key, shape, amount, slope):
    table = rank_bounds(amount, slope)
    ticket = jax.random.randint(jax.random.fold_in(stream_key, 1), shape, 0, int(table[amount - 1]))
    rank = jnp.searchsorted(jnp.asarray(table, jnp.int32), ticket, side="right")
    return jax.random.permutation(jax.random.fold_in(stream_key, 2), amount)[rank].astype(jnp.int32)


def scatter_about(rng, shape, spread, reach, shards=(), kind=jnp.bfloat16):
    values = jax.random.normal(rng, shape, jnp.float32) * spread
    if len(shards) > 0:
        values = block_levels(rng, shape, shards, -0.22, 0.18) * values
    return jnp.clip(values, min=-reach, max=reach).astype(kind)


def setup_inputs(seed: int = 0, part: int = 0) -> dict:
    arg_keys = jax.random.split(jax.random.key(seed), 8)
    own_keys = jax.random.split(jax.random.fold_in(arg_keys[7], part), 8)
    return {
        "normed_input": scatter_about(own_keys[0], (SEQ, D), 1.0, 5.0, ((0, 16),)),
        "query_base": draw_query_base(jax.random.fold_in(jax.random.fold_in(arg_keys[7], part), 71), part),
        "key_base": draw_key_base(jax.random.fold_in(jax.random.fold_in(arg_keys[7], part), 71), part),
        "value_base": scatter_about(own_keys[3], (SEQ, KEYVALUE_HEADS * HEAD_SIZE), 1.0, 4.0, ((0, 16),)),
        "adapter_pool": draw_adapter_pool(jax.random.fold_in(arg_keys[7], 71), part),
        "stretch_adapter": ranked(own_keys[5], (NCHUNK,), ADAPTERS, 2),
        "adapter_owner": jax.random.permutation(arg_keys[6], ADAPTERS).astype(jnp.int32),
    }


adapter_scale = 2.0
rope_base = 500000.0
mask_floor = -1.0e30


def rotate(delta, token_positions, heads):
    half_dim = HEAD_SIZE // 2
    frequency = rope_base ** (-(jnp.arange(half_dim, dtype=jnp.float32) * 2.0) / HEAD_SIZE)
    angle = token_positions.astype(jnp.float32)[:, None] * frequency[None, :]
    cosine = jnp.cos(angle)[:, None, :]
    sine_part = jnp.sin(angle)[:, None, :]
    shaped = delta.reshape(delta.shape[0], heads, HEAD_SIZE)
    first_half = shaped[..., :half_dim]
    second_half = shaped[..., half_dim:]
    joined = jnp.concatenate([first_half * cosine - second_half * sine_part, second_half * cosine + first_half * sine_part], -1)
    return joined.reshape(delta.shape[0], heads * HEAD_SIZE)


def adapter_inputs(hidden_state_rows, query_row_block, key_row_block, value_row_block, projection_piece, token_positions):
    split_one = D * 3 * ADAPTER_RANK
    split_two = split_one + ADAPTER_RANK * QH * HEAD_SIZE
    down_qkv = projection_piece[:split_one].reshape(D, 3 * ADAPTER_RANK)
    query_up_weight = projection_piece[split_one:split_two].reshape(ADAPTER_RANK, QH * HEAD_SIZE)
    keyvalue_up_weight = projection_piece[split_two:].reshape(ADAPTER_RANK, 2 * KEYVALUE_HEADS * HEAD_SIZE)
    narrow_product = jnp.dot(hidden_state_rows, down_qkv, preferred_element_type=jnp.float32).astype(jnp.bfloat16)
    query_correction = adapter_scale * jnp.dot(narrow_product[:, :ADAPTER_RANK], query_up_weight, preferred_element_type=jnp.float32)
    key_correction = adapter_scale * jnp.dot(narrow_product[:, ADAPTER_RANK:2 * ADAPTER_RANK], keyvalue_up_weight[:, :KEYVALUE_HEADS * HEAD_SIZE], preferred_element_type=jnp.float32)
    value_correction = adapter_scale * jnp.dot(narrow_product[:, 2 * ADAPTER_RANK:], keyvalue_up_weight[:, KEYVALUE_HEADS * HEAD_SIZE:], preferred_element_type=jnp.float32)
    queries = (query_row_block.astype(jnp.float32) + rotate(query_correction, token_positions, QH)).astype(jnp.bfloat16)
    new_keys = (key_row_block.astype(jnp.float32) + rotate(key_correction, token_positions, KEYVALUE_HEADS)).astype(jnp.bfloat16)
    new_values = (value_row_block.astype(jnp.float32) + value_correction).astype(jnp.bfloat16)
    return queries, new_keys, new_values


def output_delta(attended_rows, out_part):
    down_out = out_part[:QH * HEAD_SIZE * ADAPTER_RANK].reshape(QH * HEAD_SIZE, ADAPTER_RANK)
    raised_output = out_part[QH * HEAD_SIZE * ADAPTER_RANK:].reshape(ADAPTER_RANK, D)
    narrow_product = jnp.dot(attended_rows, down_out, preferred_element_type=jnp.float32).astype(jnp.bfloat16)
    return (adapter_scale * jnp.dot(narrow_product, raised_output, preferred_element_type=jnp.float32)).astype(jnp.bfloat16)


def reference(normed_input, query_base, key_base, value_base, adapter_pool, stretch_adapter, adapter_owner):
    adapter_ids = jnp.arange(ADAPTERS, dtype=jnp.int32)
    slots = jnp.sum(jnp.where(stretch_adapter[:, None] == adapter_ids[None, :], adapter_owner[None, :], 0), axis=1).astype(jnp.int32)

    def one_stretch(stretch_index):
        starting_row = stretch_index * BLOCK_TOKENS
        token_positions = starting_row + jnp.arange(BLOCK_TOKENS, dtype=jnp.int32)
        pool_row = lax.dynamic_index_in_dim(adapter_pool, slots[stretch_index], 0, keepdims=False)
        return adapter_inputs(lax.dynamic_slice_in_dim(normed_input, starting_row, BLOCK_TOKENS, 0),
                           lax.dynamic_slice_in_dim(query_base, starting_row, BLOCK_TOKENS, 0),
                           lax.dynamic_slice_in_dim(key_base, starting_row, BLOCK_TOKENS, 0),
                           lax.dynamic_slice_in_dim(value_base, starting_row, BLOCK_TOKENS, 0),
                           pool_row[:QKV_POOL], token_positions)

    stretch_list = jnp.arange(NCHUNK, dtype=jnp.int32)
    queries, all_keys, all_values = lax.map(one_stretch, stretch_list)
    queries = queries.reshape(SEQ, QH * HEAD_SIZE)
    key_heads = all_keys.reshape(SEQ, KEYVALUE_HEADS, HEAD_SIZE).astype(jnp.float32)
    value_heads = all_values.reshape(SEQ, KEYVALUE_HEADS, HEAD_SIZE).astype(jnp.float32)
    group_size = QH // KEYVALUE_HEADS
    block_rows = min(512, SEQ)
    key_pos = jnp.arange(SEQ, dtype=jnp.int32)

    def attend(block_index):
        starting_row = block_index * block_rows
        block_q = lax.dynamic_slice_in_dim(queries, starting_row, block_rows, 0)
        head_q = block_q.reshape(block_rows, KEYVALUE_HEADS, group_size, HEAD_SIZE).transpose(1, 2, 0, 3).reshape(KEYVALUE_HEADS, group_size * block_rows, HEAD_SIZE)
        query_pos = jnp.tile(starting_row + jnp.arange(block_rows, dtype=jnp.int32), group_size)
        scores = jnp.einsum("hqd,khd->hqk", head_q.astype(jnp.float32), key_heads) * (HEAD_SIZE ** -0.5)
        allowed = (query_pos[:, None] >= key_pos[None, :])[None]
        row_max = jnp.max(jnp.where(allowed, scores, mask_floor), axis=-1)
        weights = jnp.where(allowed, jnp.exp(scores - row_max[..., None]), 0.0)
        total = jnp.sum(weights, axis=-1)
        rounded = lax.optimization_barrier(weights.astype(jnp.bfloat16))
        summed = jnp.einsum("hqk,khd->hqd", rounded.astype(jnp.float32), value_heads)
        result = summed / total[..., None]
        return result.reshape(KEYVALUE_HEADS, group_size, block_rows, HEAD_SIZE).transpose(2, 0, 1, 3).reshape(block_rows, QH * HEAD_SIZE).astype(jnp.bfloat16)

    attended = lax.map(attend, jnp.arange(SEQ // block_rows, dtype=jnp.int32)).reshape(SEQ, QH * HEAD_SIZE)

    def out_stretch(stretch_index):
        starting_row = stretch_index * BLOCK_TOKENS
        pool_row = lax.dynamic_index_in_dim(adapter_pool, slots[stretch_index], 0, keepdims=False)
        return output_delta(lax.dynamic_slice_in_dim(attended, starting_row, BLOCK_TOKENS, 0), pool_row[QKV_POOL:])

    out_delta = lax.map(out_stretch, stretch_list).reshape(SEQ, D)
    return attended, out_delta
```

```python
from functools import partial
import math

import jax
import jax.numpy as jnp
from jax import lax
from jax.experimental import pallas as pl
from jax.experimental.pallas import tpu as pltpu
from jax.sharding import PartitionSpec as P

D = 8192
QH = 32
KEYVALUE_HEADS = 4
HEAD_SIZE = 128
ADAPTER_RANK = 64
BLOCK_TOKENS = 512
QKV_POOL = 1900544


adapter_scale = 2.0
rope_base = 500000.0
mask_floor = -1e30


LANES = 128
MESH = pl.DeviceIdType.MESH
ON_CHIP = pl.BlockSpec(memory_space=pltpu.VMEM)
SCALARS = pl.BlockSpec(memory_space=pltpu.SMEM)


def remote(src, dst, send_sem, recv_sem, group, ctx):
    return pltpu.make_async_remote_copy(
        src_ref=src,
        dst_ref=dst,
        send_sem=send_sem,
        recv_sem=recv_sem,
        device_id=(group, ctx),
        device_id_type=MESH,
    )


def place_adapter_kernel(
    groups, cubes, cube,
    pick_ref, x_ref, down_ref, rest_ref,
    x_out, down_out, rest_out,
    down_rows, rest_rows, down_send, rest_send, down_land, rest_land,
    s_cube, r_cube, s_far, r_far, s_tree, r_tree, s_own,
):
    group = lax.axis_index("groups")
    ctx = lax.axis_index("ctx")
    inner = ctx % cube
    outer = ctx // cube
    home = group * cubes + outer
    kinds = groups * cubes
    width = x_out.shape[2] // groups

    barrier = pltpu.get_barrier_semaphore()
    for k in range(1, cube):
        pl.semaphore_signal(
            barrier, inc=1, device_id=(group, outer * cube + (inner ^ k)), device_id_type=MESH
        )
    for k in range(1, kinds):
        there = home ^ k
        pl.semaphore_signal(
            barrier,
            inc=1,
            device_id=(there // cubes, (there % cubes) * cube + inner),
            device_id_type=MESH,
        )
    pl.semaphore_wait(barrier, cube - 1 + kinds - 1)

    sent = []
    down_in, rest_in, x_in = [], [], []

    def columns(part, owner):
        return pl.ds(pl.multiple_of((part * cube + owner) * width, width), width)

    for row, (source, rows, arriving) in enumerate(
        ((down_ref, down_rows, down_in), (rest_ref, rest_rows, rest_in))
    ):
        for k in reversed(range(1, cube)):
            peer = inner ^ k
            copy = remote(
                source.at[peer], rows.at[inner], s_cube.at[row, k], r_cube.at[row, k],
                group, outer * cube + peer,
            )
            copy.start()
            arriving.append(copy)
        own = pltpu.make_async_copy(source.at[inner], rows.at[inner], s_own.at[row])
        own.start()
        own.wait()
    for part in range(groups):
        for k in reversed(range(1, cube)):
            peer = inner ^ k
            copy = remote(
                x_ref.at[:, columns(part, peer)],
                x_out.at[inner, :, pl.ds(part * width, width)],
                s_cube.at[2 + part, k], r_cube.at[2 + part, k],
                group, outer * cube + peer,
            )
            copy.start()
            x_in.append(copy)
        own = pltpu.make_async_copy(
            x_ref.at[:, columns(part, inner)],
            x_out.at[inner, :, pl.ds(part * width, width)],
            s_own.at[2 + part],
        )
        own.start()
        own.wait()

    far = []
    for row, (rows, outgoing, landing, arriving) in enumerate(
        (
            (down_rows, down_send, down_land, down_in),
            (rest_rows, rest_send, rest_land, rest_in),
        )
    ):
        for copy in arriving:
            copy.wait_recv()
        coming = []
        for k in range(1, kinds):
            there = home ^ k
            outgoing[k] = rows[pick_ref[there]]
            copy = remote(
                outgoing.at[k], landing.at[k], s_far.at[row, k], r_far.at[row, k],
                there // cubes, (there % cubes) * cube + inner,
            )
            copy.start()
            coming.append(copy)
        landing[0] = rows[pick_ref[home]]
        far.append(coming)

    for copy in far[0]:
        copy.wait_recv()
    for part in range(groups):
        down_out[part] = down_land[pick_ref[kinds + part]]

    for copy in far[1]:
        copy.wait_recv()
    for part in range(groups):
        rest_out[part, inner] = rest_land[pick_ref[kinds + part]]
    sent = down_in + rest_in + x_in + far[0] + far[1]
    bit = cube // 2
    have = [0]
    tree = {}
    while bit:
        peer = outer * cube + (inner ^ bit)
        new = []
        for k in have:
            for part in range(groups):
                if k & (bit << 1):
                    tree[k, part].wait_recv()
        for k in have:
            for part in range(groups):
                slot = rest_out.at[part, inner ^ k]
                copy = remote(
                    slot, slot, s_tree.at[part, k ^ bit], r_tree.at[part, k ^ bit], group, peer
                )
                copy.start()
                tree[k ^ bit, part] = copy
            new.append(k ^ bit)
        have = have + new
        last = bit
        bit //= 2
    for key, copy in tree.items():
        if key[0] & last:
            copy.wait_recv()
        sent.append(copy)
    for copy in x_in:
        copy.wait_recv()
    for copy in sent:
        copy.wait_send()


def place_adapter(groups, cubes, cube, picks, x, down, rest):
    kinds = groups * cubes
    tokens, depth = x.shape
    down_shape, rest_shape = down.shape[1:], rest.shape[1:]
    bf16 = jnp.bfloat16
    dma = pltpu.SemaphoreType.DMA
    return pl.pallas_call(
        partial(place_adapter_kernel, groups, cubes, cube),
        out_shape=(
            jax.ShapeDtypeStruct((cube, tokens, depth // cube), bf16),
            jax.ShapeDtypeStruct((groups,) + down_shape, bf16),
            jax.ShapeDtypeStruct((groups, cube) + rest_shape, bf16),
        ),
        in_specs=[SCALARS, ON_CHIP, ON_CHIP, ON_CHIP],
        out_specs=(ON_CHIP, ON_CHIP, ON_CHIP),
        scratch_shapes=[
            pltpu.VMEM((cube,) + down_shape, bf16),
            pltpu.VMEM((cube,) + rest_shape, bf16),
            pltpu.VMEM((kinds,) + down_shape, bf16),
            pltpu.VMEM((kinds,) + rest_shape, bf16),
            pltpu.VMEM((kinds,) + down_shape, bf16),
            pltpu.VMEM((kinds,) + rest_shape, bf16),
            dma((2 + groups, cube)),
            dma((2 + groups, cube)),
            dma((2, kinds)),
            dma((2, kinds)),
            dma((groups, cube)),
            dma((groups, cube)),
            dma((2 + groups,)),
        ],
        compiler_params=pltpu.CompilerParams(
            collective_id=0, has_side_effects=True, vmem_limit_bytes=60 * 1024 * 1024
        ),
    )(picks, x, down, rest)


def narrow_kernel(cube, x_ref, w_ref, out_ref, total, outgoing, landing, s_sem, r_sem):
    group = lax.axis_index("groups")
    ctx = lax.axis_index("ctx")
    inner = ctx % cube
    outer = ctx // cube
    barrier = pltpu.get_barrier_semaphore()
    for k in range(1, cube):
        pl.semaphore_signal(
            barrier, inc=1, device_id=(group, outer * cube + (inner ^ k)), device_id_type=MESH
        )
    _, tokens, depth = x_ref.shape
    product = jnp.dot(
        x_ref[...].reshape(cube * tokens, depth), w_ref[...], preferred_element_type=jnp.float32
    ).reshape(cube, tokens, w_ref.shape[1])
    total[...] = product
    outgoing[...] = product.astype(jnp.bfloat16)
    pl.semaphore_wait(barrier, cube - 1)
    copies = []
    for k in range(1, cube):
        peer = inner ^ k
        copy = remote(
            outgoing.at[peer], landing.at[k], s_sem.at[k], r_sem.at[k], group, outer * cube + peer
        )
        copy.start()
        copies.append(copy)
    result = total[inner]
    for k, copy in zip(range(1, cube), copies):
        copy.wait_recv()
        result = result + landing[k].astype(jnp.float32)
    out_ref[...] = result.astype(jnp.bfloat16)
    for copy in copies:
        copy.wait_send()


def narrow(cube, x, w):
    _, tokens, _ = x.shape
    shape = (cube, tokens, w.shape[1])
    return pl.pallas_call(
        partial(narrow_kernel, cube),
        out_shape=jax.ShapeDtypeStruct(shape[1:], jnp.bfloat16),
        in_specs=[ON_CHIP, ON_CHIP],
        out_specs=ON_CHIP,
        scratch_shapes=[
            pltpu.VMEM(shape, jnp.float32),
            pltpu.VMEM(shape, jnp.bfloat16),
            pltpu.VMEM(shape, jnp.bfloat16),
            pltpu.SemaphoreType.DMA((cube,)),
            pltpu.SemaphoreType.DMA((cube,)),
        ],
        compiler_params=pltpu.CompilerParams(collective_id=1, has_side_effects=True),
    )(x, w)


def gather_kernel(count, kv_ref, out_ref, s_sem, r_sem, s_own):
    group = lax.axis_index("groups")
    ctx = lax.axis_index("ctx")
    barrier = pltpu.get_barrier_semaphore()
    levels = count.bit_length() - 1
    for level in range(levels):
        pl.semaphore_signal(
            barrier, inc=1, device_id=(group, ctx ^ (1 << level)), device_id_type=MESH
        )
    own = pltpu.make_async_copy(kv_ref, out_ref.at[ctx], s_own)
    own.start()
    pl.semaphore_wait(barrier, levels)
    own.wait()
    have = [0]
    copies = {}
    for level in reversed(range(levels)):
        bit = 1 << level
        new = []
        for k in have:
            if k and not k & (bit - 1) and k & (bit << 1):
                copies[k].wait_recv()
            slot = out_ref.at[ctx ^ k]
            copy = remote(slot, slot, s_sem.at[k ^ bit], r_sem.at[k ^ bit], group, ctx ^ bit)
            copy.start()
            copies[k ^ bit] = copy
            new.append(k ^ bit)
        have = have + new
    for k, copy in copies.items():
        if k & 1:
            copy.wait_recv()
    for copy in copies.values():
        copy.wait_send()


def gather_rows(count, kv):
    return pl.pallas_call(
        partial(gather_kernel, count),
        out_shape=jax.ShapeDtypeStruct((count,) + kv.shape, kv.dtype),
        in_specs=[ON_CHIP],
        out_specs=ON_CHIP,
        scratch_shapes=[
            pltpu.SemaphoreType.DMA((count,)),
            pltpu.SemaphoreType.DMA((count,)),
            pltpu.SemaphoreType.DMA,
        ],
        compiler_params=pltpu.CompilerParams(
            collective_id=2, has_side_effects=True, vmem_limit_bytes=40 * 1024 * 1024
        ),
    )(kv)


def rotate(delta, token_positions, heads):
    half_dim = HEAD_SIZE // 2
    frequency = rope_base ** (-(jnp.arange(half_dim, dtype=jnp.float32) * 2.0) / HEAD_SIZE)
    angle = token_positions.astype(jnp.float32)[:, None] * frequency[None, :]
    cosine = jnp.cos(angle)[:, None, :]
    sine_part = jnp.sin(angle)[:, None, :]
    shaped = delta.reshape(delta.shape[0], heads, HEAD_SIZE)
    first_half = shaped[..., :half_dim]
    second_half = shaped[..., half_dim:]
    joined = jnp.concatenate(
        [
            first_half * cosine - second_half * sine_part,
            second_half * cosine + first_half * sine_part,
        ],
        -1,
    )
    return joined.reshape(delta.shape[0], heads * HEAD_SIZE)


def project_heads(
    narrow_product, query_row_block, key_row_block, value_row_block, upper_part, token_positions
):
    query_up_weight = upper_part[: ADAPTER_RANK * QH * HEAD_SIZE].reshape(
        ADAPTER_RANK, QH * HEAD_SIZE
    )
    keyvalue_up_weight = upper_part[ADAPTER_RANK * QH * HEAD_SIZE :].reshape(
        ADAPTER_RANK, 2 * KEYVALUE_HEADS * HEAD_SIZE
    )
    query_correction = adapter_scale * jnp.dot(
        narrow_product[:, :ADAPTER_RANK], query_up_weight, preferred_element_type=jnp.float32
    )
    key_correction = adapter_scale * jnp.dot(
        narrow_product[:, ADAPTER_RANK : 2 * ADAPTER_RANK],
        keyvalue_up_weight[:, : KEYVALUE_HEADS * HEAD_SIZE],
        preferred_element_type=jnp.float32,
    )
    value_correction = adapter_scale * jnp.dot(
        narrow_product[:, 2 * ADAPTER_RANK :],
        keyvalue_up_weight[:, KEYVALUE_HEADS * HEAD_SIZE :],
        preferred_element_type=jnp.float32,
    )
    queries = (
        query_row_block.astype(jnp.float32) + rotate(query_correction, token_positions, QH)
    ).astype(jnp.bfloat16)
    new_keys = (
        key_row_block.astype(jnp.float32) + rotate(key_correction, token_positions, KEYVALUE_HEADS)
    ).astype(jnp.bfloat16)
    new_values = (value_row_block.astype(jnp.float32) + value_correction).astype(jnp.bfloat16)
    return (queries, new_keys, new_values)


def output_delta(attended_rows, out_part):
    down_out = out_part[: QH * HEAD_SIZE * ADAPTER_RANK].reshape(QH * HEAD_SIZE, ADAPTER_RANK)
    raised_output = out_part[QH * HEAD_SIZE * ADAPTER_RANK :].reshape(ADAPTER_RANK, D)
    narrow_product = jnp.dot(attended_rows, down_out, preferred_element_type=jnp.float32).astype(
        jnp.bfloat16
    )
    return (
        adapter_scale * jnp.dot(narrow_product, raised_output, preferred_element_type=jnp.float32)
    ).astype(jnp.bfloat16)


def head_major(query_row_block):
    count_rows = query_row_block.shape[0]
    group_size = QH // KEYVALUE_HEADS
    return (
        query_row_block.reshape(count_rows, KEYVALUE_HEADS, group_size, HEAD_SIZE)
        .transpose(1, 2, 0, 3)
        .reshape(KEYVALUE_HEADS, group_size * count_rows, HEAD_SIZE)
    )


def row_major(head_rows, count_rows):
    group_size = QH // KEYVALUE_HEADS
    return (
        head_rows.reshape(KEYVALUE_HEADS, group_size, count_rows, HEAD_SIZE)
        .transpose(2, 0, 1, 3)
        .reshape(count_rows, QH * HEAD_SIZE)
    )


def online_update(current, queries, query_pos, key_slice, value_slice, key_start):
    run_max, run_sum, run_acc = current
    scores = jnp.einsum(
        "hqd,khd->hqk", queries, key_slice, preferred_element_type=jnp.float32
    ) * HEAD_SIZE ** (-0.5)
    key_pos = key_start + jnp.arange(key_slice.shape[0], dtype=jnp.int32)
    allowed = (query_pos[:, None] >= key_pos[None, :])[None]
    new_max = jnp.maximum(run_max, jnp.max(jnp.where(allowed, scores, mask_floor), axis=-1))
    weights = jnp.where(allowed, jnp.exp(scores - new_max[..., None]), 0.0)
    rescale = jnp.exp(run_max - new_max)
    new_sum = run_sum * rescale + jnp.sum(weights, axis=-1)
    new_acc = run_acc * rescale[..., None] + jnp.einsum(
        "hqk,khd->hqd",
        weights.astype(jnp.bfloat16),
        value_slice,
        preferred_element_type=jnp.float32,
    )
    return (new_max, new_sum, new_acc)


def unchanged(current):
    return current


def fold_keys(carry_state, shard_part, prepared):
    key_row_block, value_row_block = shard_part
    key_count = key_row_block.shape[0]
    sub_width = math.gcd(key_count, 1024)
    key_heads = key_row_block.reshape(key_count // sub_width, sub_width, KEYVALUE_HEADS, HEAD_SIZE)
    value_heads = value_row_block.reshape(
        key_count // sub_width, sub_width, KEYVALUE_HEADS, HEAD_SIZE
    )

    def one_step(sub_index, carried):
        key_start = sub_index * sub_width
        key_slice = lax.dynamic_index_in_dim(key_heads, sub_index, 0, keepdims=False)
        value_slice = lax.dynamic_index_in_dim(value_heads, sub_index, 0, keepdims=False)
        updated = []
        for (queries, query_pos), running in zip(prepared, carried):
            advance = partial(
                online_update,
                queries=queries,
                query_pos=query_pos,
                key_slice=key_slice,
                value_slice=value_slice,
                key_start=key_start,
            )
            updated.append(lax.cond(key_start <= jnp.max(query_pos), advance, unchanged, running))
        return tuple(updated)

    return lax.fori_loop(0, key_count // sub_width, one_step, carry_state)


def finish_block(result, count_rows):
    run_max, run_sum, run_acc = result
    divisor = jnp.where(run_sum > 0.0, run_sum, 1.0)
    return row_major(run_acc / divisor[..., None], count_rows).astype(jnp.bfloat16)


def shards(
    normed_input, query_base, key_base, value_base, adapter_pool, stretch_adapter, adapter_owner
):
    cycle_size = lax.axis_size("ctx")
    my_index = lax.axis_index("ctx")
    tok_rows = normed_input.shape[0]
    token_positions = my_index * tok_rows + jnp.arange(tok_rows, dtype=jnp.int32)
    groups = lax.axis_size("groups")
    group = lax.axis_index("groups")
    cube = BLOCK_TOKENS // tok_rows
    cubes = cycle_size // cube
    adapter_ids = jnp.arange(adapter_owner.shape[0], dtype=jnp.int32)
    slots = jnp.sum(
        jnp.where(stretch_adapter[:, None] == adapter_ids[None, :], adapter_owner[None, :], 0),
        axis=1,
    )
    others = [slots]
    for step in range(1, groups):
        route = [(low, low ^ step) for low in range(groups)]
        others.append(lax.ppermute(slots, "groups", route))
    by_step = jnp.stack(others)
    all_slots = jnp.take(
        by_step, jnp.bitwise_xor(group, jnp.arange(groups, dtype=jnp.int32)), axis=0
    )
    my_slot = lax.dynamic_index_in_dim(slots, my_index // cube, 0, keepdims=False)
    home = group * cubes + my_index // cube
    chosen = jnp.bitwise_xor(
        jnp.arange(groups, dtype=jnp.int32) * cubes + my_slot // cube, home
    )
    picks = jnp.concatenate([(all_slots % cube).reshape(-1), chosen]).astype(jnp.int32)
    down_size = 3 * ADAPTER_RANK * D
    rest_size = adapter_pool.shape[1] - down_size
    down_part = lax.dynamic_slice_in_dim(
        adapter_pool[0], group * (down_size // groups), down_size // groups, 0
    ).reshape(cube, -1, LANES)
    rest_part = lax.dynamic_slice_in_dim(
        adapter_pool[0], down_size + group * (rest_size // groups), rest_size // groups, 0
    ).reshape(cube, -1, LANES)
    moved, down_slice, rest = place_adapter(
        groups, cubes, cube, picks, normed_input, down_part, rest_part
    )
    narrow_product = narrow(cube, moved, down_slice.reshape(D // cube, 3 * ADAPTER_RANK))
    rest_row = rest.reshape(-1)
    upper_part = rest_row[: QKV_POOL - down_size]
    out_part = rest_row[QKV_POOL - down_size :]
    queries, new_keys, new_values = project_heads(
        narrow_product, query_base, key_base, value_base, upper_part, token_positions
    )
    group_size = QH // KEYVALUE_HEADS
    blocks = [(queries, token_positions)]
    prepared = [
        (head_major(block_q), jnp.tile(block_pos, group_size)) for block_q, block_pos in blocks
    ]
    initial = tuple(
        (
            (
                jnp.full((KEYVALUE_HEADS, head_q.shape[1]), mask_floor, jnp.float32),
                jnp.zeros((KEYVALUE_HEADS, head_q.shape[1]), jnp.float32),
                jnp.zeros((KEYVALUE_HEADS, head_q.shape[1], HEAD_SIZE), jnp.float32),
            )
            for head_q, block_pos in prepared
        )
    )
    kv_width = KEYVALUE_HEADS * HEAD_SIZE
    gathered = gather_rows(cycle_size, jnp.concatenate([new_keys, new_values], axis=1)).reshape(
        cycle_size * tok_rows, 2 * kv_width
    )
    finals = fold_keys(initial, (gathered[:, :kv_width], gathered[:, kv_width:]), prepared)
    attended = finish_block(finals[0], tok_rows)
    out_delta = output_delta(attended, out_part)
    return (attended, out_delta)


def solution(mesh):
    placed = (
        P(("groups", "ctx"), None),
        P(("groups", "ctx"), None),
        P(("groups", "ctx"), None),
        P(("groups", "ctx"), None),
        P("ctx", None),
        P("groups"),
        P(),
    )
    return jax.shard_map(
        shards,
        mesh=mesh,
        in_specs=placed,
        out_specs=(P(("groups", "ctx"), None), P(("groups", "ctx"), None)),
        check_vma=False,
    )
```

```python
from functools import partial
import math

import jax
import jax.numpy as jnp
from jax import lax
from jax.experimental import pallas as pl
from jax.experimental.pallas import tpu as pltpu
from jax.sharding import PartitionSpec as P

D = 8192
QH = 32
KEYVALUE_HEADS = 4
HEAD_SIZE = 128
ADAPTER_RANK = 64
BLOCK_TOKENS = 512
QKV_POOL = 1900544


adapter_scale = 2.0
rope_base = 500000.0
mask_floor = -1e30


LANES = 128
MESH = pl.DeviceIdType.MESH
ON_CHIP = pl.BlockSpec(memory_space=pltpu.VMEM)
SCALARS = pl.BlockSpec(memory_space=pltpu.SMEM)


def remote(src, dst, send_sem, recv_sem, group, ctx):
    return pltpu.make_async_remote_copy(
        src_ref=src,
        dst_ref=dst,
        send_sem=send_sem,
        recv_sem=recv_sem,
        device_id=(group, ctx),
        device_id_type=MESH,
    )


def place_adapter_kernel(
    groups, cubes, cube, down_size,
    pick_ref, x_ref, pool_ref,
    x_out, down_out, rest_out,
    down_flat, rest_flat, down_source, rest_source,
    down_rows, rest_rows, down_send, rest_send, down_land, rest_land,
    s_flat, s_cube, r_cube, s_far, r_far, s_tree, r_tree, s_own,
):
    group = lax.axis_index("groups")
    ctx = lax.axis_index("ctx")
    inner = ctx % cube
    outer = ctx // cube
    home = group * cubes + outer
    kinds = groups * cubes
    width = x_out.shape[2] // groups
    down_piece = down_flat.shape[2]
    rest_piece = rest_flat.shape[2]

    def read_piece(row, k):
        piece = (rest_piece, down_piece)[row]
        start = (group * cube + (inner ^ k)) * piece + (down_size, 0)[row]
        return pltpu.make_async_copy(
            pool_ref.at[:, pl.ds(pl.multiple_of(start, LANES), piece)],
            (rest_flat, down_flat)[row].at[k],
            s_flat.at[row, k],
        )

    for row in range(2):
        for k in reversed(range(cube)):
            read_piece(row, k).start()

    barrier = pltpu.get_barrier_semaphore()
    for k in range(1, cube):
        pl.semaphore_signal(
            barrier, inc=1, device_id=(group, outer * cube + (inner ^ k)), device_id_type=MESH
        )
    for k in range(1, kinds):
        there = home ^ k
        pl.semaphore_signal(
            barrier,
            inc=1,
            device_id=(there // cubes, (there % cubes) * cube + inner),
            device_id_type=MESH,
        )
    pl.semaphore_wait(barrier, cube - 1 + kinds - 1)

    def columns(part, owner):
        return pl.ds(pl.multiple_of((part * cube + owner) * width, width), width)

    def cube_copy(row, k):
        peer = inner ^ k
        return remote(
            (rest_source, down_source)[row].at[k], (rest_rows, down_rows)[row].at[inner],
            s_cube.at[row, k], r_cube.at[row, k], group, outer * cube + peer,
        )

    def dense(row, k):
        flat = (rest_flat, down_flat)[row][k].astype(jnp.float32)
        return flat.reshape(-1, LANES).astype(jnp.bfloat16)

    def x_copy(part, k):
        peer = inner ^ k
        return remote(
            x_ref.at[:, columns(part, peer)],
            x_out.at[inner, :, pl.ds(part * width, width)],
            s_cube.at[2 + part, k], r_cube.at[2 + part, k],
            group, outer * cube + peer,
        )

    for row, (source, rows) in enumerate(((rest_source, rest_rows), (down_source, down_rows))):

        def spread(step, carry, row=row, source=source):
            k = cube - 1 - step
            read_piece(row, k).wait()
            source[k] = dense(row, k)
            cube_copy(row, k).start()
            return carry

        lax.fori_loop(0, cube - 1, spread, 0)
        read_piece(row, 0).wait()
        rows[inner] = dense(row, 0)

    owns = []
    for part in range(groups):
        own = pltpu.make_async_copy(
            x_ref.at[:, columns(part, inner)],
            x_out.at[inner, :, pl.ds(part * width, width)],
            s_own.at[part],
        )
        own.start()
        owns.append(own)

    far = []
    for row, (rows, outgoing, landing) in enumerate(
        ((rest_rows, rest_send, rest_land), (down_rows, down_send, down_land))
    ):
        for k in range(1, cube):
            cube_copy(row, k).wait_recv()
        coming = []
        for k in range(1, kinds):
            there = home ^ k
            outgoing[k] = rows[pick_ref[there]]
            copy = remote(
                outgoing.at[k], landing.at[k], s_far.at[row, k], r_far.at[row, k],
                there // cubes, (there % cubes) * cube + inner,
            )
            copy.start()
            coming.append(copy)
        landing[0] = rows[pick_ref[home]]
        far.append(coming)

    for copy in far[0]:
        copy.wait_recv()
    for part in range(groups):
        rest_out[part, inner] = rest_land[pick_ref[kinds + part]]
    tree = {}
    have = [[0] for _ in range(groups)]
    levels = cube.bit_length() - 1
    orders = []
    for part in range(groups):
        order = [1 << level for level in reversed(range(levels))]
        if part % 2:
            order[:2] = order[1::-1]
        orders.append(order)
    for stage in range(levels):
        for part in range(groups):
            bit = orders[part][stage]
            before = orders[part][stage - 1] if stage else 0
            for k in have[part]:
                if k & before:
                    tree[k, part].wait_recv()
            new = []
            for k in have[part]:
                slot = rest_out.at[part, inner ^ k]
                copy = remote(
                    slot, slot, s_tree.at[part, k ^ bit], r_tree.at[part, k ^ bit],
                    group, outer * cube + (inner ^ bit),
                )
                copy.start()
                tree[k ^ bit, part] = copy
                new.append(k ^ bit)
            have[part] = have[part] + new
        if stage == 0:
            for part in range(groups):
                for k in reversed(range(1, cube)):
                    x_copy(part, k).start()

    for copy in far[1]:
        copy.wait_recv()
    for part in range(groups):
        down_out[part] = down_land[pick_ref[kinds + part]]
    for (k, part), copy in tree.items():
        if k & orders[part][-1]:
            copy.wait_recv()
    for own in owns:
        own.wait()
    for part in range(groups):
        for k in range(1, cube):
            x_copy(part, k).wait_recv()
            x_copy(part, k).wait_send()
    for row in range(2):
        for k in range(1, cube):
            cube_copy(row, k).wait_send()
    for copy in far[0] + far[1] + list(tree.values()):
        copy.wait_send()


def place_adapter(groups, cubes, cube, down_size, picks, x, pool):
    kinds = groups * cubes
    tokens, depth = x.shape
    down_piece = down_size // (groups * cube)
    rest_piece = (pool.shape[1] - down_size) // (groups * cube)
    down_shape = (down_piece // LANES, LANES)
    rest_shape = (rest_piece // LANES, LANES)
    bf16 = jnp.bfloat16
    dma = pltpu.SemaphoreType.DMA
    return pl.pallas_call(
        partial(place_adapter_kernel, groups, cubes, cube, down_size),
        out_shape=(
            jax.ShapeDtypeStruct((cube, tokens, depth // cube), bf16),
            jax.ShapeDtypeStruct((groups,) + down_shape, bf16),
            jax.ShapeDtypeStruct((groups, cube) + rest_shape, bf16),
        ),
        in_specs=[SCALARS, ON_CHIP, pl.BlockSpec(memory_space=pl.ANY)],
        out_specs=(ON_CHIP, ON_CHIP, ON_CHIP),
        scratch_shapes=[
            pltpu.VMEM((cube, 1, down_piece), bf16),
            pltpu.VMEM((cube, 1, rest_piece), bf16),
            pltpu.VMEM((cube,) + down_shape, bf16),
            pltpu.VMEM((cube,) + rest_shape, bf16),
            pltpu.VMEM((cube,) + down_shape, bf16),
            pltpu.VMEM((cube,) + rest_shape, bf16),
            pltpu.VMEM((kinds,) + down_shape, bf16),
            pltpu.VMEM((kinds,) + rest_shape, bf16),
            pltpu.VMEM((kinds,) + down_shape, bf16),
            pltpu.VMEM((kinds,) + rest_shape, bf16),
            dma((2, cube)),
            dma((2 + groups, cube)),
            dma((2 + groups, cube)),
            dma((2, kinds)),
            dma((2, kinds)),
            dma((groups, cube)),
            dma((groups, cube)),
            dma((groups,)),
        ],
        compiler_params=pltpu.CompilerParams(
            collective_id=0, has_side_effects=True, vmem_limit_bytes=60 * 1024 * 1024
        ),
    )(picks, x, pool)


def keyval_kernel(
    cube, count,
    x_ref, w_ref, up_ref, key_ref, value_ref, cos_ref, sin_ref,
    narrow_out, out_ref,
    total, outgoing, landing, s_sem, r_sem, s_all, r_all,
):
    group = lax.axis_index("groups")
    ctx = lax.axis_index("ctx")
    inner = ctx % cube
    outer = ctx // cube
    levels = count.bit_length() - 1
    barrier = pltpu.get_barrier_semaphore()
    apart = list(range(1, cube)) + [1 << n for n in range(levels) if 1 << n >= cube]
    for k in apart:
        pl.semaphore_signal(barrier, inc=1, device_id=(group, ctx ^ k), device_id_type=MESH)
    _, tokens, depth = x_ref.shape
    product = jnp.dot(
        x_ref[...].reshape(cube * tokens, depth), w_ref[...], preferred_element_type=jnp.float32
    ).reshape(cube, tokens, w_ref.shape[1])
    total[...] = product
    outgoing[...] = product.astype(jnp.bfloat16)
    pl.semaphore_wait(barrier, len(apart))
    copies = []
    for k in range(1, cube):
        peer = inner ^ k
        copy = remote(
            outgoing.at[peer], landing.at[k], s_sem.at[k], r_sem.at[k], group, outer * cube + peer
        )
        copy.start()
        copies.append(copy)
    result = total[inner]
    for k, copy in zip(range(1, cube), copies):
        copy.wait_recv()
        result = result + landing[k].astype(jnp.float32)
    low = result.astype(jnp.bfloat16)
    narrow_out[...] = low
    half = HEAD_SIZE // 2
    for j in range(2 * KEYVALUE_HEADS):
        first = ADAPTER_RANK * (1 if j < KEYVALUE_HEADS else 2)
        delta = adapter_scale * jnp.dot(
            low[:, first : first + ADAPTER_RANK], up_ref[j], preferred_element_type=jnp.float32
        )
        base_ref = key_ref if j < KEYVALUE_HEADS else value_ref
        head = j % KEYVALUE_HEADS
        if j < KEYVALUE_HEADS:
            swapped = jnp.concatenate([delta[:, half:], delta[:, :half]], axis=1)
            delta = delta * cos_ref[...] + swapped * sin_ref[...]
        base = base_ref[:, head * HEAD_SIZE : (head + 1) * HEAD_SIZE].astype(jnp.float32)
        out_ref[ctx, :, j * HEAD_SIZE : (j + 1) * HEAD_SIZE] = (base + delta).astype(jnp.bfloat16)
    have = [0]
    moved = {}
    for level in reversed(range(levels)):
        bit = 1 << level
        new = []
        for k in have:
            if k & (bit << 1):
                moved[k].wait_recv()
            slot = out_ref.at[ctx ^ k]
            copy = remote(slot, slot, s_all.at[k ^ bit], r_all.at[k ^ bit], group, ctx ^ bit)
            copy.start()
            moved[k ^ bit] = copy
            new.append(k ^ bit)
        have = have + new
    for k, copy in moved.items():
        if k & 1:
            copy.wait_recv()
    for copy in copies + list(moved.values()):
        copy.wait_send()


def keyval(cube, count, x, w, up, key_rows, value_rows, cosine, sine):
    _, tokens, _ = x.shape
    shape = (cube, tokens, w.shape[1])
    dma = pltpu.SemaphoreType.DMA
    return pl.pallas_call(
        partial(keyval_kernel, cube, count),
        out_shape=(
            jax.ShapeDtypeStruct(shape[1:], jnp.bfloat16),
            jax.ShapeDtypeStruct(
                (count, tokens, 2 * KEYVALUE_HEADS * HEAD_SIZE), jnp.bfloat16
            ),
        ),
        in_specs=[ON_CHIP] * 7,
        out_specs=(ON_CHIP, ON_CHIP),
        scratch_shapes=[
            pltpu.VMEM(shape, jnp.float32),
            pltpu.VMEM(shape, jnp.bfloat16),
            pltpu.VMEM(shape, jnp.bfloat16),
            dma((cube,)),
            dma((cube,)),
            dma((count,)),
            dma((count,)),
        ],
        compiler_params=pltpu.CompilerParams(
            collective_id=1, has_side_effects=True, vmem_limit_bytes=40 * 1024 * 1024
        ),
    )(x, w, up, key_rows, value_rows, cosine, sine)


def attend_kernel(
    step_keys, narrow_ref, query_ref, kv_ref, rest_ref, cos_ref, sin_ref,
    attended_ref, delta_ref,
    wide, queries, permuted, run_max, run_sum, run_acc,
):
    tokens = narrow_ref.shape[0]
    ctx = lax.axis_index("ctx")
    heads = QH // KEYVALUE_HEADS
    rows = heads * tokens
    half = HEAD_SIZE // 2
    query_rows = ADAPTER_RANK * QH
    out_start = query_rows + 2 * ADAPTER_RANK * KEYVALUE_HEADS
    raise_start = out_start + QH * half
    wide[...] = rest_ref[...].astype(jnp.float32)
    low = narrow_ref[:, :ADAPTER_RANK]
    for head in range(QH):
        up = wide[pl.ds(head, ADAPTER_RANK, stride=QH), :].astype(jnp.bfloat16)
        delta = adapter_scale * jnp.dot(low, up, preferred_element_type=jnp.float32)
        delta = delta * cos_ref[...] + pltpu.roll(delta, half, 1) * sin_ref[...]
        base = query_ref[:, head * HEAD_SIZE : (head + 1) * HEAD_SIZE].astype(jnp.float32)
        queries[head // heads, pl.ds((head % heads) * tokens, tokens), :] = (base + delta).astype(
            jnp.bfloat16
        )
    first = ctx * tokens
    steps = (first + tokens + step_keys - 1) // step_keys
    row = lax.broadcasted_iota(jnp.int32, (rows, step_keys), 0)
    query_pos = first + lax.rem(row, tokens)
    key_off = lax.broadcasted_iota(jnp.int32, (rows, step_keys), 1)
    source = lax.broadcasted_iota(jnp.int32, (HEAD_SIZE, HEAD_SIZE), 0)
    target = lax.broadcasted_iota(jnp.int32, (HEAD_SIZE, HEAD_SIZE), 1)
    wanted = jnp.where(target < half, 2 * target, 2 * (target - half) + 1)
    shuffle = jnp.where(source == wanted, 1.0, 0.0).astype(jnp.bfloat16)
    for group in range(KEYVALUE_HEADS):
        run_max[...] = jnp.full_like(run_max, mask_floor)
        run_sum[...] = jnp.zeros_like(run_sum)
        run_acc[...] = jnp.zeros_like(run_acc)
        key_cols = slice(group * HEAD_SIZE, (group + 1) * HEAD_SIZE)
        value_first = (KEYVALUE_HEADS + group) * HEAD_SIZE

        def advance(step, carry):
            start = pl.multiple_of(step * step_keys, step_keys)
            keys = kv_ref[pl.ds(start, step_keys), key_cols]
            values = kv_ref[pl.ds(start, step_keys), value_first : value_first + HEAD_SIZE]
            scores = lax.dot_general(
                queries[group], keys, (((1,), (1,)), ((), ())),
                preferred_element_type=jnp.float32,
            ) * HEAD_SIZE ** (-0.5)
            scores = jnp.where(query_pos >= key_off + start, scores, mask_floor)
            new_max = jnp.maximum(run_max[...], jnp.max(scores, axis=1, keepdims=True))
            weights = jnp.exp(scores - new_max)
            rescale = jnp.exp(run_max[...] - new_max)
            run_sum[...] = run_sum[...] * rescale + jnp.sum(weights, axis=1, keepdims=True)
            run_acc[...] = run_acc[...] * rescale + jnp.dot(
                weights.astype(jnp.bfloat16), values, preferred_element_type=jnp.float32
            )
            run_max[...] = new_max
            return carry

        lax.fori_loop(0, steps, advance, 0)
        result = (run_acc[...] / run_sum[...]).astype(jnp.bfloat16)
        mixed = jnp.dot(result, shuffle, preferred_element_type=jnp.float32).astype(jnp.bfloat16)
        for j in range(heads):
            head = group * heads + j
            cols = slice(head * HEAD_SIZE, (head + 1) * HEAD_SIZE)
            attended_ref[:, cols] = result[j * tokens : (j + 1) * tokens]
            permuted[:, cols] = mixed[j * tokens : (j + 1) * tokens]
    narrow = jnp.zeros((tokens, ADAPTER_RANK), jnp.float32)
    for head in range(QH):
        block = rest_ref[out_start + head * half : out_start + (head + 1) * half, :]
        weight = jnp.concatenate([block[:, :half], block[:, half:]], axis=0)
        narrow = narrow + jnp.dot(
            permuted[:, head * HEAD_SIZE : (head + 1) * HEAD_SIZE],
            weight,
            preferred_element_type=jnp.float32,
        )
    narrow = narrow.astype(jnp.bfloat16)
    blocks = D // LANES
    for j in range(blocks):
        up = wide[pl.ds(raise_start + j, ADAPTER_RANK, stride=blocks), :].astype(jnp.bfloat16)
        delta_ref[:, j * LANES : (j + 1) * LANES] = (
            adapter_scale * jnp.dot(narrow, up, preferred_element_type=jnp.float32)
        ).astype(jnp.bfloat16)


def attend(narrow, query_rows, kv, rest, cosine, sine):
    tokens = narrow.shape[0]
    rows = QH // KEYVALUE_HEADS * tokens
    return pl.pallas_call(
        partial(attend_kernel, math.gcd(kv.shape[0], 1024)),
        out_shape=(
            jax.ShapeDtypeStruct((tokens, QH * HEAD_SIZE), jnp.bfloat16),
            jax.ShapeDtypeStruct((tokens, D), jnp.bfloat16),
        ),
        in_specs=[ON_CHIP] * 6,
        out_specs=(ON_CHIP, ON_CHIP),
        scratch_shapes=[
            pltpu.VMEM(rest.shape, jnp.float32),
            pltpu.VMEM((KEYVALUE_HEADS, rows, HEAD_SIZE), jnp.bfloat16),
            pltpu.VMEM((tokens, QH * HEAD_SIZE), jnp.bfloat16),
            pltpu.VMEM((rows, 1), jnp.float32),
            pltpu.VMEM((rows, 1), jnp.float32),
            pltpu.VMEM((rows, HEAD_SIZE), jnp.float32),
        ],
        compiler_params=pltpu.CompilerParams(vmem_limit_bytes=56 * 1024 * 1024),
    )(narrow, query_rows, kv, rest, cosine, sine)


def shards(
    normed_input, query_base, key_base, value_base, adapter_pool, stretch_adapter, adapter_owner
):
    cycle_size = lax.axis_size("ctx")
    my_index = lax.axis_index("ctx")
    tok_rows = normed_input.shape[0]
    token_positions = my_index * tok_rows + jnp.arange(tok_rows, dtype=jnp.int32)
    groups = lax.axis_size("groups")
    group = lax.axis_index("groups")
    cube = BLOCK_TOKENS // tok_rows
    cubes = cycle_size // cube
    adapter_ids = jnp.arange(adapter_owner.shape[0], dtype=jnp.int32)
    slots = jnp.sum(
        jnp.where(stretch_adapter[:, None] == adapter_ids[None, :], adapter_owner[None, :], 0),
        axis=1,
    )
    others = [slots]
    for step in range(1, groups):
        route = [(low, low ^ step) for low in range(groups)]
        others.append(lax.ppermute(slots, "groups", route))
    by_step = jnp.stack(others)
    all_slots = jnp.take(
        by_step, jnp.bitwise_xor(group, jnp.arange(groups, dtype=jnp.int32)), axis=0
    )
    my_slot = lax.dynamic_index_in_dim(slots, my_index // cube, 0, keepdims=False)
    home = group * cubes + my_index // cube
    chosen = jnp.bitwise_xor(
        jnp.arange(groups, dtype=jnp.int32) * cubes + my_slot // cube, home
    )
    picks = jnp.concatenate([(all_slots % cube).reshape(-1), chosen]).astype(jnp.int32)
    down_size = 3 * ADAPTER_RANK * D
    half_dim = HEAD_SIZE // 2
    frequency = rope_base ** (-(jnp.arange(half_dim, dtype=jnp.float32) * 2.0) / HEAD_SIZE)
    angle = token_positions.astype(jnp.float32)[:, None] * frequency[None, :]
    cosine = jnp.cos(angle)
    sine = jnp.sin(angle)
    cosine = jnp.concatenate([cosine, cosine], axis=1)
    sine = jnp.concatenate([-sine, sine], axis=1)
    moved, down_slice, rest = place_adapter(
        groups, cubes, cube, down_size, picks, normed_input, adapter_pool
    )
    rest = rest.reshape(-1, LANES)
    query_part = ADAPTER_RANK * QH
    keyval_up = (
        rest[query_part : query_part + 2 * ADAPTER_RANK * KEYVALUE_HEADS]
        .reshape(ADAPTER_RANK, 2 * KEYVALUE_HEADS, LANES)
        .transpose(1, 0, 2)
    )
    narrow_product, gathered = keyval(
        cube,
        cycle_size,
        moved,
        down_slice.reshape(D // cube, 3 * ADAPTER_RANK),
        keyval_up,
        key_base,
        value_base,
        cosine,
        sine,
    )
    gathered = gathered.reshape(cycle_size * tok_rows, -1)
    return attend(narrow_product, query_base, gathered, rest, cosine, sine)


def solution(mesh):
    placed = (
        P(("groups", "ctx"), None),
        P(("groups", "ctx"), None),
        P(("groups", "ctx"), None),
        P(("groups", "ctx"), None),
        P("ctx", None),
        P("groups"),
        P(),
    )
    return jax.shard_map(
        shards,
        mesh=mesh,
        in_specs=placed,
        out_specs=(P(("groups", "ctx"), None), P(("groups", "ctx"), None)),
        check_vma=False,
    )
```

```python
from functools import partial
import math

import jax
import jax.numpy as jnp
from jax import lax
from jax.experimental import pallas as pl
from jax.experimental.pallas import tpu as pltpu
from jax.sharding import PartitionSpec as P

D = 8192
QH = 32
KEYVALUE_HEADS = 4
HEAD_SIZE = 128
ADAPTER_RANK = 64
BLOCK_TOKENS = 512
QKV_POOL = 1900544


adapter_scale = 2.0
rope_base = 500000.0
mask_floor = -1e30


LANES = 128
MESH = pl.DeviceIdType.MESH
ON_CHIP = pl.BlockSpec(memory_space=pltpu.VMEM)
SCALARS = pl.BlockSpec(memory_space=pltpu.SMEM)


def remote(src, dst, send_sem, recv_sem, group, ctx):
    return pltpu.make_async_remote_copy(
        src_ref=src,
        dst_ref=dst,
        send_sem=send_sem,
        recv_sem=recv_sem,
        device_id=(group, ctx),
        device_id_type=MESH,
    )


def place_adapter_kernel(
    groups, cubes, cube, down_size,
    owner_ref, stretch_ref, x_ref, pool_ref,
    x_out, down_out, rest_out,
    down_flat, rest_flat, down_source, rest_source,
    down_rows, rest_rows, down_send, rest_send, down_land, rest_land,
    stretch_land, table,
    s_flat, s_cube, r_cube, s_far, r_far, s_tree, r_tree, s_own, s_row, r_row, s_table,
):
    group = lax.axis_index("groups")
    ctx = lax.axis_index("ctx")
    inner = ctx % cube
    outer = ctx // cube
    home = group * cubes + outer
    kinds = groups * cubes
    width = x_out.shape[2] // groups
    down_piece = down_flat.shape[2]
    rest_piece = rest_flat.shape[2]

    def read_piece(row, k):
        piece = (rest_piece, down_piece)[row]
        start = (group * cube + (inner ^ k)) * piece + (down_size, 0)[row]
        return pltpu.make_async_copy(
            pool_ref.at[:, pl.ds(pl.multiple_of(start, LANES), piece)],
            (rest_flat, down_flat)[row].at[k],
            s_flat.at[row, k],
        )

    for row in range(2):
        for k in reversed(range(cube)):
            read_piece(row, k).start()

    barrier = pltpu.get_barrier_semaphore()
    for k in range(1, cube):
        pl.semaphore_signal(
            barrier, inc=1, device_id=(group, outer * cube + (inner ^ k)), device_id_type=MESH
        )
    for k in range(1, kinds):
        there = home ^ k
        pl.semaphore_signal(
            barrier,
            inc=1,
            device_id=(there // cubes, (there % cubes) * cube + inner),
            device_id_type=MESH,
        )
    pl.semaphore_wait(barrier, cube - 1 + kinds - 1)
    row_copies = []
    for step in range(1, groups):
        copy = remote(
            stretch_ref, stretch_land.at[step], s_row.at[step], r_row.at[step], group ^ step, ctx
        )
        copy.start()
        row_copies.append(copy)

    def columns(part, owner):
        return pl.ds(pl.multiple_of((part * cube + owner) * width, width), width)

    def cube_copy(row, k):
        peer = inner ^ k
        return remote(
            (rest_source, down_source)[row].at[k], (rest_rows, down_rows)[row].at[inner],
            s_cube.at[row, k], r_cube.at[row, k], group, outer * cube + peer,
        )

    def dense(row, k):
        flat = (rest_flat, down_flat)[row][k].astype(jnp.float32)
        return flat.reshape(-1, LANES).astype(jnp.bfloat16)

    def x_copy(part, k):
        peer = inner ^ k
        return remote(
            x_ref.at[:, columns(part, peer)],
            x_out.at[inner, :, pl.ds(part * width, width)],
            s_cube.at[2 + part, k], r_cube.at[2 + part, k],
            group, outer * cube + peer,
        )

    for row, (source, rows) in enumerate(((rest_source, rest_rows), (down_source, down_rows))):

        def spread(step, carry, row=row, source=source):
            k = cube - 1 - step
            read_piece(row, k).wait()
            source[k] = dense(row, k)
            cube_copy(row, k).start()
            return carry

        lax.fori_loop(0, cube - 1, spread, 0)
        read_piece(row, 0).wait()
        rows[inner] = dense(row, 0)

    to_table = [pltpu.make_async_copy(stretch_ref, table.at[0], s_table.at[0])]
    to_table[0].start()
    for step, copy in zip(range(1, groups), row_copies):
        copy.wait_recv()
        move = pltpu.make_async_copy(stretch_land.at[step], table.at[step], s_table.at[step])
        move.start()
        to_table.append(move)
    for move in to_table:
        move.wait()

    def slot_of(k):
        return owner_ref[table[k // cubes, 0, outer ^ (k % cubes)]]

    def chosen(part):
        return (part * cubes + lax.div(slot_of(0), cube)) ^ home

    owns = []
    for part in range(groups):
        own = pltpu.make_async_copy(
            x_ref.at[:, columns(part, inner)],
            x_out.at[inner, :, pl.ds(part * width, width)],
            s_own.at[part],
        )
        own.start()
        owns.append(own)

    far = []
    for row, (rows, outgoing, landing) in enumerate(
        ((rest_rows, rest_send, rest_land), (down_rows, down_send, down_land))
    ):
        for k in range(1, cube):
            cube_copy(row, k).wait_recv()
        coming = []
        for k in range(1, kinds):
            there = home ^ k
            outgoing[k] = rows[lax.rem(slot_of(k), cube)]
            copy = remote(
                outgoing.at[k], landing.at[k], s_far.at[row, k], r_far.at[row, k],
                there // cubes, (there % cubes) * cube + inner,
            )
            copy.start()
            coming.append(copy)
        landing[0] = rows[lax.rem(slot_of(0), cube)]
        far.append(coming)

    for copy in far[0]:
        copy.wait_recv()
    for part in range(groups):
        rest_out[part, inner] = rest_land[chosen(part)]
    tree = {}
    have = [[0] for _ in range(groups)]
    levels = cube.bit_length() - 1
    orders = []
    for part in range(groups):
        order = [1 << level for level in reversed(range(levels))]
        if part % 2:
            order[:2] = order[1::-1]
        orders.append(order)
    for stage in range(levels):
        for part in range(groups):
            bit = orders[part][stage]
            before = orders[part][stage - 1] if stage else 0
            for k in have[part]:
                if k & before:
                    tree[k, part].wait_recv()
            new = []
            for k in have[part]:
                slot = rest_out.at[part, inner ^ k]
                copy = remote(
                    slot, slot, s_tree.at[part, k ^ bit], r_tree.at[part, k ^ bit],
                    group, outer * cube + (inner ^ bit),
                )
                copy.start()
                tree[k ^ bit, part] = copy
                new.append(k ^ bit)
            have[part] = have[part] + new
        if stage == 0:
            for part in range(groups):
                for k in reversed(range(1, cube)):
                    x_copy(part, k).start()

    for copy in far[1]:
        copy.wait_recv()
    for part in range(groups):
        down_out[part] = down_land[chosen(part)]
    for (k, part), copy in tree.items():
        if k & orders[part][-1]:
            copy.wait_recv()
    for own in owns:
        own.wait()
    for part in range(groups):
        for k in range(1, cube):
            x_copy(part, k).wait_recv()
            x_copy(part, k).wait_send()
    for row in range(2):
        for k in range(1, cube):
            cube_copy(row, k).wait_send()
    for copy in row_copies + far[0] + far[1] + list(tree.values()):
        copy.wait_send()


def place_adapter(groups, cubes, cube, down_size, owner, stretch_row, x, pool):
    kinds = groups * cubes
    tokens, depth = x.shape
    down_piece = down_size // (groups * cube)
    rest_piece = (pool.shape[1] - down_size) // (groups * cube)
    down_shape = (down_piece // LANES, LANES)
    rest_shape = (rest_piece // LANES, LANES)
    bf16 = jnp.bfloat16
    dma = pltpu.SemaphoreType.DMA
    return pl.pallas_call(
        partial(place_adapter_kernel, groups, cubes, cube, down_size),
        out_shape=(
            jax.ShapeDtypeStruct((cube, tokens, depth // cube), bf16),
            jax.ShapeDtypeStruct((groups,) + down_shape, bf16),
            jax.ShapeDtypeStruct((groups, cube) + rest_shape, bf16),
        ),
        in_specs=[SCALARS, ON_CHIP, ON_CHIP, pl.BlockSpec(memory_space=pl.ANY)],
        out_specs=(ON_CHIP, ON_CHIP, ON_CHIP),
        scratch_shapes=[
            pltpu.VMEM((cube, 1, down_piece), bf16),
            pltpu.VMEM((cube, 1, rest_piece), bf16),
            pltpu.VMEM((cube,) + down_shape, bf16),
            pltpu.VMEM((cube,) + rest_shape, bf16),
            pltpu.VMEM((cube,) + down_shape, bf16),
            pltpu.VMEM((cube,) + rest_shape, bf16),
            pltpu.VMEM((kinds,) + down_shape, bf16),
            pltpu.VMEM((kinds,) + rest_shape, bf16),
            pltpu.VMEM((kinds,) + down_shape, bf16),
            pltpu.VMEM((kinds,) + rest_shape, bf16),
            pltpu.VMEM((groups,) + stretch_row.shape, jnp.int32),
            pltpu.SMEM((groups,) + stretch_row.shape, jnp.int32),
            dma((2, cube)),
            dma((2 + groups, cube)),
            dma((2 + groups, cube)),
            dma((2, kinds)),
            dma((2, kinds)),
            dma((groups, cube)),
            dma((groups, cube)),
            dma((groups,)),
            dma((groups,)),
            dma((groups,)),
            dma((groups,)),
        ],
        compiler_params=pltpu.CompilerParams(
            collective_id=0, has_side_effects=True, vmem_limit_bytes=60 * 1024 * 1024
        ),
    )(owner, stretch_row, x, pool)


def keyval_kernel(
    cube, count,
    x_ref, w_ref, up_ref, query_ref, key_ref, value_ref, cos_ref, sin_ref,
    query_out, out_ref,
    wide, total, outgoing, landing, s_sem, r_sem, s_all, r_all,
):
    group = lax.axis_index("groups")
    ctx = lax.axis_index("ctx")
    inner = ctx % cube
    outer = ctx // cube
    levels = count.bit_length() - 1
    barrier = pltpu.get_barrier_semaphore()
    apart = list(range(1, cube)) + [1 << n for n in range(levels) if 1 << n >= cube]
    for k in apart:
        pl.semaphore_signal(barrier, inc=1, device_id=(group, ctx ^ k), device_id_type=MESH)
    _, tokens, depth = x_ref.shape
    product = jnp.dot(
        x_ref[...].reshape(cube * tokens, depth), w_ref[...], preferred_element_type=jnp.float32
    ).reshape(cube, tokens, w_ref.shape[1])
    total[...] = product
    outgoing[...] = product.astype(jnp.bfloat16)
    pl.semaphore_wait(barrier, len(apart))
    copies = []
    for k in range(1, cube):
        peer = inner ^ k
        copy = remote(
            outgoing.at[peer], landing.at[k], s_sem.at[k], r_sem.at[k], group, outer * cube + peer
        )
        copy.start()
        copies.append(copy)
    wide[...] = up_ref[: wide.shape[0], :].astype(jnp.float32)
    result = total[inner]
    for k, copy in zip(range(1, cube), copies):
        copy.wait_recv()
        result = result + landing[k].astype(jnp.float32)
    low = result.astype(jnp.bfloat16)
    half = HEAD_SIZE // 2
    query_rows = ADAPTER_RANK * QH
    kinds = 2 * KEYVALUE_HEADS
    for j in range(2 * KEYVALUE_HEADS):
        first = ADAPTER_RANK * (1 if j < KEYVALUE_HEADS else 2)
        delta = adapter_scale * jnp.dot(
            low[:, first : first + ADAPTER_RANK],
            wide[pl.ds(query_rows + j, ADAPTER_RANK, stride=kinds), :].astype(jnp.bfloat16),
            preferred_element_type=jnp.float32
        )
        base_ref = key_ref if j < KEYVALUE_HEADS else value_ref
        head = j % KEYVALUE_HEADS
        if j < KEYVALUE_HEADS:
            swapped = jnp.concatenate([delta[:, half:], delta[:, :half]], axis=1)
            delta = delta * cos_ref[...] + swapped * sin_ref[...]
        base = base_ref[:, head * HEAD_SIZE : (head + 1) * HEAD_SIZE].astype(jnp.float32)
        out_ref[ctx, :, j * HEAD_SIZE : (j + 1) * HEAD_SIZE] = (base + delta).astype(jnp.bfloat16)

    def query_head(head):
        up = wide[pl.ds(head, ADAPTER_RANK, stride=QH), :].astype(jnp.bfloat16)
        delta = adapter_scale * jnp.dot(
            low[:, :ADAPTER_RANK], up, preferred_element_type=jnp.float32
        )
        swapped = jnp.concatenate([delta[:, half:], delta[:, :half]], axis=1)
        delta = delta * cos_ref[...] + swapped * sin_ref[...]
        base = query_ref[:, head * HEAD_SIZE : (head + 1) * HEAD_SIZE].astype(jnp.float32)
        shared = QH // KEYVALUE_HEADS
        query_out[
            head // shared, (head % shared) * tokens : (head % shared + 1) * tokens, :
        ] = (base + delta).astype(jnp.bfloat16)

    kv_width = KEYVALUE_HEADS * HEAD_SIZE
    far_first = [1 << level for level in reversed(range(levels))]
    orders = (far_first, [2] + [bit for bit in far_first if bit != 2])
    have = [[0], [0]]
    moved = {}
    done = 0
    for stage in range(levels):
        for part in range(2):
            bit = orders[part][stage]
            before = orders[part][stage - 1] if stage else 0
            new = []
            for k in have[part]:
                if k & before:
                    moved[k, part].wait_recv()
                slot = out_ref.at[ctx ^ k, :, pl.ds(part * kv_width, kv_width)]
                copy = remote(
                    slot, slot, s_all.at[part, k ^ bit], r_all.at[part, k ^ bit], group, ctx ^ bit
                )
                copy.start()
                moved[k ^ bit, part] = copy
                new.append(k ^ bit)
            have[part] = have[part] + new
        until = QH * (stage + 1) // levels
        for head in range(done, until):
            query_head(head)
        done = until
    for (k, part), copy in moved.items():
        if k & orders[part][-1]:
            copy.wait_recv()
    for copy in copies + list(moved.values()):
        copy.wait_send()


def keyval(cube, count, x, w, rest, query_rows, key_rows, value_rows, cosine, sine):
    _, tokens, _ = x.shape
    shape = (cube, tokens, w.shape[1])
    up_rows = ADAPTER_RANK * (QH + 2 * KEYVALUE_HEADS)
    dma = pltpu.SemaphoreType.DMA
    return pl.pallas_call(
        partial(keyval_kernel, cube, count),
        out_shape=(
            jax.ShapeDtypeStruct(
                (KEYVALUE_HEADS, QH // KEYVALUE_HEADS * tokens, HEAD_SIZE), jnp.bfloat16
            ),
            jax.ShapeDtypeStruct(
                (count, tokens, 2 * KEYVALUE_HEADS * HEAD_SIZE), jnp.bfloat16
            ),
        ),
        in_specs=[ON_CHIP] * 8,
        out_specs=(ON_CHIP, ON_CHIP),
        scratch_shapes=[
            pltpu.VMEM((up_rows, LANES), jnp.float32),
            pltpu.VMEM(shape, jnp.float32),
            pltpu.VMEM(shape, jnp.bfloat16),
            pltpu.VMEM(shape, jnp.bfloat16),
            dma((cube,)),
            dma((cube,)),
            dma((2, count)),
            dma((2, count)),
        ],
        compiler_params=pltpu.CompilerParams(
            collective_id=1, has_side_effects=True, vmem_limit_bytes=40 * 1024 * 1024
        ),
    )(x, w, rest, query_rows, key_rows, value_rows, cosine, sine)


def attend_kernel(
    step_keys, queries, kv_ref, rest_ref,
    attended_ref, delta_ref,
    wide, permuted, run_max, run_sum, run_acc,
):
    tokens = attended_ref.shape[0]
    ctx = lax.axis_index("ctx")
    heads = QH // KEYVALUE_HEADS
    rows = heads * tokens
    half = HEAD_SIZE // 2
    query_rows = ADAPTER_RANK * QH
    out_start = query_rows + 2 * ADAPTER_RANK * KEYVALUE_HEADS
    raise_start = out_start + QH * half
    wide[...] = rest_ref[raise_start:, :].astype(jnp.float32)
    first = ctx * tokens
    steps = (first + tokens + step_keys - 1) // step_keys
    row = lax.broadcasted_iota(jnp.int32, (rows, step_keys), 0)
    query_pos = first + lax.rem(row, tokens)
    key_off = lax.broadcasted_iota(jnp.int32, (rows, step_keys), 1)
    source = lax.broadcasted_iota(jnp.int32, (HEAD_SIZE, HEAD_SIZE), 0)
    target = lax.broadcasted_iota(jnp.int32, (HEAD_SIZE, HEAD_SIZE), 1)
    wanted = jnp.where(target < half, 2 * target, 2 * (target - half) + 1)
    shuffle = jnp.where(source == wanted, 1.0, 0.0).astype(jnp.bfloat16)
    for group in range(KEYVALUE_HEADS):
        run_max[...] = jnp.full_like(run_max, mask_floor)
        run_sum[...] = jnp.zeros_like(run_sum)
        run_acc[...] = jnp.zeros_like(run_acc)
        key_cols = slice(group * HEAD_SIZE, (group + 1) * HEAD_SIZE)
        value_first = (KEYVALUE_HEADS + group) * HEAD_SIZE

        def advance(step, carry):
            start = pl.multiple_of(step * step_keys, step_keys)
            keys = kv_ref[pl.ds(start, step_keys), key_cols]
            values = kv_ref[pl.ds(start, step_keys), value_first : value_first + HEAD_SIZE]
            scores = lax.dot_general(
                queries[group], keys, (((1,), (1,)), ((), ())),
                preferred_element_type=jnp.float32,
            ) * HEAD_SIZE ** (-0.5)
            scores = jnp.where(query_pos >= key_off + start, scores, mask_floor)
            new_max = jnp.maximum(run_max[...], jnp.max(scores, axis=1, keepdims=True))
            weights = jnp.exp(scores - new_max)
            rescale = jnp.exp(run_max[...] - new_max)
            run_sum[...] = run_sum[...] * rescale + jnp.sum(weights, axis=1, keepdims=True)
            run_acc[...] = run_acc[...] * rescale + jnp.dot(
                weights.astype(jnp.bfloat16), values, preferred_element_type=jnp.float32
            )
            run_max[...] = new_max
            return carry

        lax.fori_loop(0, steps, advance, 0)
        result = (run_acc[...] / run_sum[...]).astype(jnp.bfloat16)
        mixed = jnp.dot(result, shuffle, preferred_element_type=jnp.float32).astype(jnp.bfloat16)
        for j in range(heads):
            head = group * heads + j
            cols = slice(head * HEAD_SIZE, (head + 1) * HEAD_SIZE)
            attended_ref[:, cols] = result[j * tokens : (j + 1) * tokens]
            permuted[:, cols] = mixed[j * tokens : (j + 1) * tokens]
    narrow = jnp.zeros((tokens, ADAPTER_RANK), jnp.float32)
    for head in range(QH):
        block = rest_ref[out_start + head * half : out_start + (head + 1) * half, :]
        weight = jnp.concatenate([block[:, :half], block[:, half:]], axis=0)
        narrow = narrow + jnp.dot(
            permuted[:, head * HEAD_SIZE : (head + 1) * HEAD_SIZE],
            weight,
            preferred_element_type=jnp.float32,
        )
    narrow = narrow.astype(jnp.bfloat16)
    blocks = D // LANES
    for j in range(blocks):
        up = wide[pl.ds(j, ADAPTER_RANK, stride=blocks), :].astype(jnp.bfloat16)
        delta_ref[:, j * LANES : (j + 1) * LANES] = (
            adapter_scale * jnp.dot(narrow, up, preferred_element_type=jnp.float32)
        ).astype(jnp.bfloat16)


def attend(queries, kv, rest):
    rows = queries.shape[1]
    tokens = rows // (QH // KEYVALUE_HEADS)
    return pl.pallas_call(
        partial(attend_kernel, math.gcd(kv.shape[0], 1024)),
        out_shape=(
            jax.ShapeDtypeStruct((tokens, QH * HEAD_SIZE), jnp.bfloat16),
            jax.ShapeDtypeStruct((tokens, D), jnp.bfloat16),
        ),
        in_specs=[ON_CHIP] * 3,
        out_specs=(ON_CHIP, ON_CHIP),
        scratch_shapes=[
            pltpu.VMEM((ADAPTER_RANK * D // LANES, LANES), jnp.float32),
            pltpu.VMEM((tokens, QH * HEAD_SIZE), jnp.bfloat16),
            pltpu.VMEM((rows, 1), jnp.float32),
            pltpu.VMEM((rows, 1), jnp.float32),
            pltpu.VMEM((rows, HEAD_SIZE), jnp.float32),
        ],
        compiler_params=pltpu.CompilerParams(vmem_limit_bytes=56 * 1024 * 1024),
    )(queries, kv, rest)


def shards(
    normed_input, query_base, key_base, value_base, adapter_pool, stretch_adapter, adapter_owner
):
    cycle_size = lax.axis_size("ctx")
    my_index = lax.axis_index("ctx")
    tok_rows = normed_input.shape[0]
    token_positions = my_index * tok_rows + jnp.arange(tok_rows, dtype=jnp.int32)
    groups = lax.axis_size("groups")
    cube = BLOCK_TOKENS // tok_rows
    cubes = cycle_size // cube
    padding = -stretch_adapter.shape[0] % LANES
    stretch_row = jnp.pad(stretch_adapter, (0, padding))[None]
    down_size = 3 * ADAPTER_RANK * D
    half_dim = HEAD_SIZE // 2
    frequency = rope_base ** (-(jnp.arange(half_dim, dtype=jnp.float32) * 2.0) / HEAD_SIZE)
    angle = token_positions.astype(jnp.float32)[:, None] * frequency[None, :]
    cosine = jnp.cos(angle)
    sine = jnp.sin(angle)
    cosine = jnp.concatenate([cosine, cosine], axis=1)
    sine = jnp.concatenate([-sine, sine], axis=1)
    moved, down_slice, rest = place_adapter(
        groups, cubes, cube, down_size, adapter_owner, stretch_row, normed_input, adapter_pool
    )
    rest = rest.reshape(-1, LANES)
    queries, gathered = keyval(
        cube,
        cycle_size,
        moved,
        down_slice.reshape(D // cube, 3 * ADAPTER_RANK),
        rest,
        query_base,
        key_base,
        value_base,
        cosine,
        sine,
    )
    gathered = gathered.reshape(cycle_size * tok_rows, -1)
    return attend(queries, gathered, rest)


def solution(mesh):
    placed = (
        P(("groups", "ctx"), None),
        P(("groups", "ctx"), None),
        P(("groups", "ctx"), None),
        P(("groups", "ctx"), None),
        P("ctx", None),
        P("groups"),
        P(),
    )
    return jax.shard_map(
        shards,
        mesh=mesh,
        in_specs=placed,
        out_specs=(P(("groups", "ctx"), None), P(("groups", "ctx"), None)),
        check_vma=False,
    )
```

```python
from functools import partial
import math

import jax
import jax.numpy as jnp
from jax import lax
from jax.experimental import pallas as pl
from jax.experimental.pallas import tpu as pltpu
from jax.sharding import PartitionSpec as P

D = 8192
QH = 32
KEYVALUE_HEADS = 4
HEAD_SIZE = 128
ADAPTER_RANK = 64
BLOCK_TOKENS = 512
QKV_POOL = 1900544


adapter_scale = 2.0
rope_base = 500000.0
mask_floor = -1e30


LANES = 128
MESH = pl.DeviceIdType.MESH
ON_CHIP = pl.BlockSpec(memory_space=pltpu.VMEM)
ANYWHERE = pl.BlockSpec(memory_space=pl.ANY)
SCALARS = pl.BlockSpec(memory_space=pltpu.SMEM)


def remote(src, dst, send_sem, recv_sem, group, ctx):
    return pltpu.make_async_remote_copy(
        src_ref=src,
        dst_ref=dst,
        send_sem=send_sem,
        recv_sem=recv_sem,
        device_id=(group, ctx),
        device_id_type=MESH,
    )


def place_adapter_kernel(
    groups, cubes, cube, down_size,
    owner_ref, stretch_ref, x_ref, pool_ref,
    x_out, down_out, rest_out,
    down_flat, rest_flat, down_source, rest_source,
    down_rows, rest_rows, down_send, rest_send, down_land, rest_land,
    stretch_land, table,
    s_flat, s_cube, r_cube, s_far, r_far, s_tree, r_tree, s_own, s_row, r_row, s_table,
):
    group = lax.axis_index("groups")
    ctx = lax.axis_index("ctx")
    inner = ctx % cube
    outer = ctx // cube
    home = group * cubes + outer
    kinds = groups * cubes
    width = x_out.shape[2] // groups
    down_piece = down_flat.shape[2]
    rest_piece = rest_flat.shape[2]

    def read_piece(row, k):
        piece = (rest_piece, down_piece)[row]
        start = (group * cube + (inner ^ k)) * piece + (down_size, 0)[row]
        return pltpu.make_async_copy(
            pool_ref.at[:, pl.ds(pl.multiple_of(start, LANES), piece)],
            (rest_flat, down_flat)[row].at[k],
            s_flat.at[row, k],
        )

    for row in range(2):
        for k in reversed(range(cube)):
            read_piece(row, k).start()

    barrier = pltpu.get_barrier_semaphore()
    for k in range(1, cube):
        pl.semaphore_signal(
            barrier, inc=1, device_id=(group, outer * cube + (inner ^ k)), device_id_type=MESH
        )
    for k in range(1, kinds):
        there = home ^ k
        pl.semaphore_signal(
            barrier,
            inc=1,
            device_id=(there // cubes, (there % cubes) * cube + inner),
            device_id_type=MESH,
        )
    pl.semaphore_wait(barrier, cube - 1 + kinds - 1)
    row_copies = []
    for step in range(1, groups):
        copy = remote(
            stretch_ref, stretch_land.at[step], s_row.at[step], r_row.at[step], group ^ step, ctx
        )
        copy.start()
        row_copies.append(copy)

    def columns(part, owner):
        return pl.ds(pl.multiple_of((part * cube + owner) * width, width), width)

    def cube_copy(row, k):
        peer = inner ^ k
        return remote(
            (rest_source, down_source)[row].at[k], (rest_rows, down_rows)[row].at[inner],
            s_cube.at[row, k], r_cube.at[row, k], group, outer * cube + peer,
        )

    def dense(row, k):
        flat = (rest_flat, down_flat)[row][k].astype(jnp.float32)
        return flat.reshape(-1, LANES).astype(jnp.bfloat16)

    def x_copy(part, k):
        peer = inner ^ k
        return remote(
            x_ref.at[:, columns(part, peer)],
            x_out.at[inner, :, pl.ds(part * width, width)],
            s_cube.at[2 + part, k], r_cube.at[2 + part, k],
            group, outer * cube + peer,
        )

    for row, (source, rows) in enumerate(((rest_source, rest_rows), (down_source, down_rows))):

        def spread(step, carry, row=row, source=source):
            k = cube - 1 - step
            read_piece(row, k).wait()
            source[k] = dense(row, k)
            cube_copy(row, k).start()
            return carry

        lax.fori_loop(0, cube - 1, spread, 0)
        read_piece(row, 0).wait()
        rows[inner] = dense(row, 0)

    to_table = [pltpu.make_async_copy(stretch_ref, table.at[0], s_table.at[0])]
    to_table[0].start()
    for step, copy in zip(range(1, groups), row_copies):
        copy.wait_recv()
        move = pltpu.make_async_copy(stretch_land.at[step], table.at[step], s_table.at[step])
        move.start()
        to_table.append(move)
    for move in to_table:
        move.wait()

    def slot_of(k):
        return owner_ref[table[k // cubes, 0, outer ^ (k % cubes)]]

    def chosen(part):
        return (part * cubes + lax.div(slot_of(0), cube)) ^ home

    owns = []
    for part in range(groups):
        own = pltpu.make_async_copy(
            x_ref.at[:, columns(part, inner)],
            x_out.at[inner, :, pl.ds(part * width, width)],
            s_own.at[part],
        )
        own.start()
        owns.append(own)

    far = []
    for row, (rows, outgoing, landing) in enumerate(
        ((rest_rows, rest_send, rest_land), (down_rows, down_send, down_land))
    ):
        for k in range(1, cube):
            cube_copy(row, k).wait_recv()
        coming = []
        for k in range(1, kinds):
            there = home ^ k
            outgoing[k] = rows[lax.rem(slot_of(k), cube)]
            copy = remote(
                outgoing.at[k], landing.at[k], s_far.at[row, k], r_far.at[row, k],
                there // cubes, (there % cubes) * cube + inner,
            )
            copy.start()
            coming.append(copy)
        landing[0] = rows[lax.rem(slot_of(0), cube)]
        far.append(coming)

    for copy in far[0]:
        copy.wait_recv()
    for part in range(groups):
        rest_out[part, inner] = rest_land[chosen(part)]
    tree = {}
    have = [[0] for _ in range(groups)]
    levels = cube.bit_length() - 1
    orders = []
    for part in range(groups):
        order = [1 << level for level in reversed(range(levels))]
        if part % 2:
            order[:2] = order[1::-1]
        orders.append(order)
    for stage in range(levels):
        for part in range(groups):
            bit = orders[part][stage]
            before = orders[part][stage - 1] if stage else 0
            for k in have[part]:
                if k & before:
                    tree[k, part].wait_recv()
            new = []
            for k in have[part]:
                slot = rest_out.at[part, inner ^ k]
                copy = remote(
                    slot, slot, s_tree.at[part, k ^ bit], r_tree.at[part, k ^ bit],
                    group, outer * cube + (inner ^ bit),
                )
                copy.start()
                tree[k ^ bit, part] = copy
                new.append(k ^ bit)
            have[part] = have[part] + new
        if stage == 0:
            for part in range(groups):
                for k in reversed(range(1, cube)):
                    x_copy(part, k).start()

    for copy in far[1]:
        copy.wait_recv()
    for part in range(groups):
        down_out[part] = down_land[chosen(part)]
    for (k, part), copy in tree.items():
        if k & orders[part][-1]:
            copy.wait_recv()
    for own in owns:
        own.wait()
    for part in range(groups):
        for k in range(1, cube):
            x_copy(part, k).wait_recv()
            x_copy(part, k).wait_send()
    for row in range(2):
        for k in range(1, cube):
            cube_copy(row, k).wait_send()
    for copy in row_copies + far[0] + far[1] + list(tree.values()):
        copy.wait_send()


def place_adapter(groups, cubes, cube, down_size, owner, stretch_row, x, pool):
    kinds = groups * cubes
    tokens, depth = x.shape
    down_piece = down_size // (groups * cube)
    rest_piece = (pool.shape[1] - down_size) // (groups * cube)
    down_shape = (down_piece // LANES, LANES)
    rest_shape = (rest_piece // LANES, LANES)
    bf16 = jnp.bfloat16
    dma = pltpu.SemaphoreType.DMA
    return pl.pallas_call(
        partial(place_adapter_kernel, groups, cubes, cube, down_size),
        out_shape=(
            jax.ShapeDtypeStruct((cube, tokens, depth // cube), bf16),
            jax.ShapeDtypeStruct((groups,) + down_shape, bf16),
            jax.ShapeDtypeStruct((groups, cube) + rest_shape, bf16),
        ),
        in_specs=[SCALARS, ON_CHIP, ON_CHIP, pl.BlockSpec(memory_space=pl.ANY)],
        out_specs=(ON_CHIP, ON_CHIP, ON_CHIP),
        scratch_shapes=[
            pltpu.VMEM((cube, 1, down_piece), bf16),
            pltpu.VMEM((cube, 1, rest_piece), bf16),
            pltpu.VMEM((cube,) + down_shape, bf16),
            pltpu.VMEM((cube,) + rest_shape, bf16),
            pltpu.VMEM((cube,) + down_shape, bf16),
            pltpu.VMEM((cube,) + rest_shape, bf16),
            pltpu.VMEM((kinds,) + down_shape, bf16),
            pltpu.VMEM((kinds,) + rest_shape, bf16),
            pltpu.VMEM((kinds,) + down_shape, bf16),
            pltpu.VMEM((kinds,) + rest_shape, bf16),
            pltpu.VMEM((groups,) + stretch_row.shape, jnp.int32),
            pltpu.SMEM((groups,) + stretch_row.shape, jnp.int32),
            dma((2, cube)),
            dma((2 + groups, cube)),
            dma((2 + groups, cube)),
            dma((2, kinds)),
            dma((2, kinds)),
            dma((groups, cube)),
            dma((groups, cube)),
            dma((groups,)),
            dma((groups,)),
            dma((groups,)),
            dma((groups,)),
        ],
        compiler_params=pltpu.CompilerParams(
            collective_id=0, has_side_effects=True, vmem_limit_bytes=60 * 1024 * 1024
        ),
    )(owner, stretch_row, x, pool)


def keyval_kernel(
    cube, count,
    x_any, w_ref, rest_any, query_ref, key_ref, value_ref, cos_ref, sin_ref,
    query_out, out_ref,
    x_ref, up_ref, s_in, wide, total, outgoing, landing, s_sem, r_sem, s_all, r_all,
):
    group = lax.axis_index("groups")
    ctx = lax.axis_index("ctx")
    inner = ctx % cube
    outer = ctx // cube
    levels = count.bit_length() - 1
    x_in = pltpu.make_async_copy(x_any, x_ref, s_in.at[0])
    x_in.start()
    up_in = pltpu.make_async_copy(
        rest_any.at[pl.ds(0, up_ref.shape[0])], up_ref, s_in.at[1]
    )
    up_in.start()
    barrier = pltpu.get_barrier_semaphore()
    apart = list(range(1, cube)) + [1 << n for n in range(levels) if 1 << n >= cube]
    for k in apart:
        pl.semaphore_signal(barrier, inc=1, device_id=(group, ctx ^ k), device_id_type=MESH)
    _, tokens, depth = x_ref.shape
    x_in.wait()
    product = jnp.dot(
        x_ref[...].reshape(cube * tokens, depth), w_ref[...], preferred_element_type=jnp.float32
    ).reshape(cube, tokens, w_ref.shape[1])
    total[...] = product
    outgoing[...] = product.astype(jnp.bfloat16)
    pl.semaphore_wait(barrier, len(apart))
    copies = []
    for k in range(1, cube):
        peer = inner ^ k
        copy = remote(
            outgoing.at[peer], landing.at[k], s_sem.at[k], r_sem.at[k], group, outer * cube + peer
        )
        copy.start()
        copies.append(copy)
    up_in.wait()
    wide[...] = up_ref[...].astype(jnp.float32)
    result = total[inner]
    for k, copy in zip(range(1, cube), copies):
        copy.wait_recv()
        result = result + landing[k].astype(jnp.float32)
    low = result.astype(jnp.bfloat16)
    half = HEAD_SIZE // 2
    query_rows = ADAPTER_RANK * QH
    kinds = 2 * KEYVALUE_HEADS
    for j in range(2 * KEYVALUE_HEADS):
        first = ADAPTER_RANK * (1 if j < KEYVALUE_HEADS else 2)
        delta = adapter_scale * jnp.dot(
            low[:, first : first + ADAPTER_RANK],
            wide[pl.ds(query_rows + j, ADAPTER_RANK, stride=kinds), :].astype(jnp.bfloat16),
            preferred_element_type=jnp.float32
        )
        base_ref = key_ref if j < KEYVALUE_HEADS else value_ref
        head = j % KEYVALUE_HEADS
        if j < KEYVALUE_HEADS:
            swapped = jnp.concatenate([delta[:, half:], delta[:, :half]], axis=1)
            delta = delta * cos_ref[...] + swapped * sin_ref[...]
        base = base_ref[:, head * HEAD_SIZE : (head + 1) * HEAD_SIZE].astype(jnp.float32)
        out_ref[ctx, :, j * HEAD_SIZE : (j + 1) * HEAD_SIZE] = (base + delta).astype(jnp.bfloat16)

    def query_head(head):
        up = wide[pl.ds(head, ADAPTER_RANK, stride=QH), :].astype(jnp.bfloat16)
        delta = adapter_scale * jnp.dot(
            low[:, :ADAPTER_RANK], up, preferred_element_type=jnp.float32
        )
        swapped = jnp.concatenate([delta[:, half:], delta[:, :half]], axis=1)
        delta = delta * cos_ref[...] + swapped * sin_ref[...]
        base = query_ref[:, head * HEAD_SIZE : (head + 1) * HEAD_SIZE].astype(jnp.float32)
        shared = QH // KEYVALUE_HEADS
        query_out[
            head // shared, (head % shared) * tokens : (head % shared + 1) * tokens, :
        ] = (base + delta).astype(jnp.bfloat16)

    kv_width = KEYVALUE_HEADS * HEAD_SIZE
    far_first = [1 << level for level in reversed(range(levels))]
    orders = (far_first, [2] + [bit for bit in far_first if bit != 2])
    have = [[0], [0]]
    moved = {}
    done = 0
    for stage in range(levels):
        for part in range(2):
            bit = orders[part][stage]
            before = orders[part][stage - 1] if stage else 0
            new = []
            for k in have[part]:
                if k & before:
                    moved[k, part].wait_recv()
                slot = out_ref.at[ctx ^ k, :, pl.ds(part * kv_width, kv_width)]
                copy = remote(
                    slot, slot, s_all.at[part, k ^ bit], r_all.at[part, k ^ bit], group, ctx ^ bit
                )
                copy.start()
                moved[k ^ bit, part] = copy
                new.append(k ^ bit)
            have[part] = have[part] + new
        until = QH * (stage + 1) // levels
        for head in range(done, until):
            query_head(head)
        done = until
    for (k, part), copy in moved.items():
        if k & orders[part][-1]:
            copy.wait_recv()
    for copy in copies + list(moved.values()):
        copy.wait_send()


def keyval(cube, count, x, w, rest, query_rows, key_rows, value_rows, cosine, sine):
    _, tokens, _ = x.shape
    shape = (cube, tokens, w.shape[1])
    up_rows = ADAPTER_RANK * (QH + 2 * KEYVALUE_HEADS)
    dma = pltpu.SemaphoreType.DMA
    return pl.pallas_call(
        partial(keyval_kernel, cube, count),
        out_shape=(
            jax.ShapeDtypeStruct(
                (KEYVALUE_HEADS, QH // KEYVALUE_HEADS * tokens, HEAD_SIZE), jnp.bfloat16
            ),
            jax.ShapeDtypeStruct(
                (count, tokens, 2 * KEYVALUE_HEADS * HEAD_SIZE), jnp.bfloat16
            ),
        ),
        in_specs=[ANYWHERE, ON_CHIP, ANYWHERE] + [ON_CHIP] * 5,
        out_specs=(ON_CHIP, ON_CHIP),
        scratch_shapes=[
            pltpu.VMEM(x.shape, jnp.bfloat16),
            pltpu.VMEM((up_rows, LANES), jnp.bfloat16),
            dma((2,)),
            pltpu.VMEM((up_rows, LANES), jnp.float32),
            pltpu.VMEM(shape, jnp.float32),
            pltpu.VMEM(shape, jnp.bfloat16),
            pltpu.VMEM(shape, jnp.bfloat16),
            dma((cube,)),
            dma((cube,)),
            dma((2, count)),
            dma((2, count)),
        ],
        compiler_params=pltpu.CompilerParams(
            collective_id=1, has_side_effects=True, vmem_limit_bytes=40 * 1024 * 1024
        ),
    )(x, w, rest, query_rows, key_rows, value_rows, cosine, sine)


def attend_kernel(
    step_keys, queries, kv_ref, rest_any,
    attended_ref, delta_ref,
    rest_ref, s_in, wide, permuted, run_max, run_sum, run_acc,
):
    tokens = attended_ref.shape[0]
    ctx = lax.axis_index("ctx")
    heads = QH // KEYVALUE_HEADS
    rows = heads * tokens
    half = HEAD_SIZE // 2
    query_rows = ADAPTER_RANK * QH
    raise_start = QH * half
    rest_in = pltpu.make_async_copy(
        rest_any.at[pl.ds(query_rows + 2 * ADAPTER_RANK * KEYVALUE_HEADS, rest_ref.shape[0])],
        rest_ref,
        s_in,
    )
    rest_in.start()
    first = ctx * tokens
    steps = (first + tokens + step_keys - 1) // step_keys
    row = lax.broadcasted_iota(jnp.int32, (rows, step_keys), 0)
    query_pos = first + lax.rem(row, tokens)
    key_off = lax.broadcasted_iota(jnp.int32, (rows, step_keys), 1)
    source = lax.broadcasted_iota(jnp.int32, (HEAD_SIZE, HEAD_SIZE), 0)
    target = lax.broadcasted_iota(jnp.int32, (HEAD_SIZE, HEAD_SIZE), 1)
    wanted = jnp.where(target < half, 2 * target, 2 * (target - half) + 1)
    shuffle = jnp.where(source == wanted, 1.0, 0.0).astype(jnp.bfloat16)
    for group in range(KEYVALUE_HEADS):
        run_max[...] = jnp.full_like(run_max, mask_floor)
        run_sum[...] = jnp.zeros_like(run_sum)
        run_acc[...] = jnp.zeros_like(run_acc)
        key_cols = slice(group * HEAD_SIZE, (group + 1) * HEAD_SIZE)
        value_first = (KEYVALUE_HEADS + group) * HEAD_SIZE

        def advance(step, carry):
            start = pl.multiple_of(step * step_keys, step_keys)
            keys = kv_ref[pl.ds(start, step_keys), key_cols]
            values = kv_ref[pl.ds(start, step_keys), value_first : value_first + HEAD_SIZE]
            scores = lax.dot_general(
                queries[group], keys, (((1,), (1,)), ((), ())),
                preferred_element_type=jnp.float32,
            ) * HEAD_SIZE ** (-0.5)
            scores = jnp.where(query_pos >= key_off + start, scores, mask_floor)
            new_max = jnp.maximum(run_max[...], jnp.max(scores, axis=1, keepdims=True))
            weights = jnp.exp(scores - new_max)
            rescale = jnp.exp(run_max[...] - new_max)
            run_sum[...] = run_sum[...] * rescale + jnp.sum(weights, axis=1, keepdims=True)
            run_acc[...] = run_acc[...] * rescale + jnp.dot(
                weights.astype(jnp.bfloat16), values, preferred_element_type=jnp.float32
            )
            run_max[...] = new_max
            return carry

        lax.fori_loop(0, steps, advance, 0)
        result = (run_acc[...] / run_sum[...]).astype(jnp.bfloat16)
        mixed = jnp.dot(result, shuffle, preferred_element_type=jnp.float32).astype(jnp.bfloat16)
        for j in range(heads):
            head = group * heads + j
            cols = slice(head * HEAD_SIZE, (head + 1) * HEAD_SIZE)
            attended_ref[:, cols] = result[j * tokens : (j + 1) * tokens]
            permuted[:, cols] = mixed[j * tokens : (j + 1) * tokens]
    rest_in.wait()
    wide[...] = rest_ref[raise_start:, :].astype(jnp.float32)
    narrow = jnp.zeros((tokens, ADAPTER_RANK), jnp.float32)
    for head in range(QH):
        block = rest_ref[head * half : (head + 1) * half, :]
        weight = jnp.concatenate([block[:, :half], block[:, half:]], axis=0)
        narrow = narrow + jnp.dot(
            permuted[:, head * HEAD_SIZE : (head + 1) * HEAD_SIZE],
            weight,
            preferred_element_type=jnp.float32,
        )
    narrow = narrow.astype(jnp.bfloat16)
    blocks = D // LANES
    for j in range(blocks):
        up = wide[pl.ds(j, ADAPTER_RANK, stride=blocks), :].astype(jnp.bfloat16)
        delta_ref[:, j * LANES : (j + 1) * LANES] = (
            adapter_scale * jnp.dot(narrow, up, preferred_element_type=jnp.float32)
        ).astype(jnp.bfloat16)


def attend(queries, kv, rest):
    rows = queries.shape[1]
    tokens = rows // (QH // KEYVALUE_HEADS)
    out_rows = ADAPTER_RANK * (QH * HEAD_SIZE + D) // LANES
    return pl.pallas_call(
        partial(attend_kernel, math.gcd(kv.shape[0], 1024)),
        out_shape=(
            jax.ShapeDtypeStruct((tokens, QH * HEAD_SIZE), jnp.bfloat16),
            jax.ShapeDtypeStruct((tokens, D), jnp.bfloat16),
        ),
        in_specs=[ON_CHIP, ON_CHIP, ANYWHERE],
        out_specs=(ON_CHIP, ON_CHIP),
        scratch_shapes=[
            pltpu.VMEM((out_rows, LANES), jnp.bfloat16),
            pltpu.SemaphoreType.DMA,
            pltpu.VMEM((ADAPTER_RANK * D // LANES, LANES), jnp.float32),
            pltpu.VMEM((tokens, QH * HEAD_SIZE), jnp.bfloat16),
            pltpu.VMEM((rows, 1), jnp.float32),
            pltpu.VMEM((rows, 1), jnp.float32),
            pltpu.VMEM((rows, HEAD_SIZE), jnp.float32),
        ],
        compiler_params=pltpu.CompilerParams(vmem_limit_bytes=56 * 1024 * 1024),
    )(queries, kv, rest)


def shards(
    normed_input, query_base, key_base, value_base, adapter_pool, stretch_adapter, adapter_owner
):
    cycle_size = lax.axis_size("ctx")
    my_index = lax.axis_index("ctx")
    tok_rows = normed_input.shape[0]
    token_positions = my_index * tok_rows + jnp.arange(tok_rows, dtype=jnp.int32)
    groups = lax.axis_size("groups")
    cube = BLOCK_TOKENS // tok_rows
    cubes = cycle_size // cube
    padding = -stretch_adapter.shape[0] % LANES
    stretch_row = jnp.pad(stretch_adapter, (0, padding))[None]
    down_size = 3 * ADAPTER_RANK * D
    half_dim = HEAD_SIZE // 2
    frequency = rope_base ** (-(jnp.arange(half_dim, dtype=jnp.float32) * 2.0) / HEAD_SIZE)
    angle = token_positions.astype(jnp.float32)[:, None] * frequency[None, :]
    cosine = jnp.cos(angle)
    sine = jnp.sin(angle)
    cosine = jnp.concatenate([cosine, cosine], axis=1)
    sine = jnp.concatenate([-sine, sine], axis=1)
    moved, down_slice, rest = place_adapter(
        groups, cubes, cube, down_size, adapter_owner, stretch_row, normed_input, adapter_pool
    )
    rest = rest.reshape(-1, LANES)
    queries, gathered = keyval(
        cube,
        cycle_size,
        moved,
        down_slice.reshape(D // cube, 3 * ADAPTER_RANK),
        rest,
        query_base,
        key_base,
        value_base,
        cosine,
        sine,
    )
    gathered = gathered.reshape(cycle_size * tok_rows, -1)
    return attend(queries, gathered, rest)


def solution(mesh):
    placed = (
        P(("groups", "ctx"), None),
        P(("groups", "ctx"), None),
        P(("groups", "ctx"), None),
        P(("groups", "ctx"), None),
        P("ctx", None),
        P("groups"),
        P(),
    )
    return jax.shard_map(
        shards,
        mesh=mesh,
        in_specs=placed,
        out_specs=(P(("groups", "ctx"), None), P(("groups", "ctx"), None)),
        check_vma=False,
    )
```

```python
from functools import partial
import math

import jax
import jax.numpy as jnp
from jax import lax
from jax.experimental import pallas as pl
from jax.experimental.pallas import tpu as pltpu
from jax.sharding import PartitionSpec as P

D = 8192
QH = 32
KEYVALUE_HEADS = 4
HEAD_SIZE = 128
ADAPTER_RANK = 64
BLOCK_TOKENS = 512
QKV_POOL = 1900544


adapter_scale = 2.0
rope_base = 500000.0
mask_floor = -1e30


LANES = 128
MESH = pl.DeviceIdType.MESH
ON_CHIP = pl.BlockSpec(memory_space=pltpu.VMEM)
ANYWHERE = pl.BlockSpec(memory_space=pl.ANY)
SCALARS = pl.BlockSpec(memory_space=pltpu.SMEM)


def remote(src, dst, send_sem, recv_sem, group, ctx):
    return pltpu.make_async_remote_copy(
        src_ref=src,
        dst_ref=dst,
        send_sem=send_sem,
        recv_sem=recv_sem,
        device_id=(group, ctx),
        device_id_type=MESH,
    )


def place_adapter_kernel(
    groups, cubes, cube, down_size,
    owner_ref, stretch_ref, x_ref, pool_ref,
    x_out, down_out, rest_out,
    down_flat, rest_flat, down_source, rest_source,
    down_rows, rest_rows, down_send, rest_send, down_land, rest_land,
    stretch_land, table,
    s_flat, s_cube, r_cube, s_far, r_far, s_tree, r_tree, s_own, s_row, r_row, s_table,
):
    group = lax.axis_index("groups")
    ctx = lax.axis_index("ctx")
    inner = ctx % cube
    outer = ctx // cube
    home = group * cubes + outer
    kinds = groups * cubes
    width = x_out.shape[2] // groups
    down_piece = down_flat.shape[2]
    rest_piece = rest_flat.shape[2]

    def read_piece(row, k):
        piece = (rest_piece, down_piece)[row]
        start = (group * cube + (inner ^ k)) * piece + (down_size, 0)[row]
        return pltpu.make_async_copy(
            pool_ref.at[:, pl.ds(pl.multiple_of(start, LANES), piece)],
            (rest_flat, down_flat)[row].at[k],
            s_flat.at[row, k],
        )

    for row in range(2):
        for k in reversed(range(cube)):
            read_piece(row, k).start()

    barrier = pltpu.get_barrier_semaphore()
    for k in range(1, cube):
        pl.semaphore_signal(
            barrier, inc=1, device_id=(group, outer * cube + (inner ^ k)), device_id_type=MESH
        )
    for k in range(1, kinds):
        there = home ^ k
        pl.semaphore_signal(
            barrier,
            inc=1,
            device_id=(there // cubes, (there % cubes) * cube + inner),
            device_id_type=MESH,
        )
    pl.semaphore_wait(barrier, cube - 1 + kinds - 1)
    row_copies = []
    for step in range(1, groups):
        copy = remote(
            stretch_ref, stretch_land.at[step], s_row.at[step], r_row.at[step], group ^ step, ctx
        )
        copy.start()
        row_copies.append(copy)

    def columns(part, owner):
        return pl.ds(pl.multiple_of((part * cube + owner) * width, width), width)

    def cube_copy(row, k):
        peer = inner ^ k
        return remote(
            (rest_source, down_source)[row].at[k], (rest_rows, down_rows)[row].at[inner],
            s_cube.at[row, k], r_cube.at[row, k], group, outer * cube + peer,
        )

    def dense(row, k):
        flat = (rest_flat, down_flat)[row][k].astype(jnp.float32)
        return flat.reshape(-1, LANES).astype(jnp.bfloat16)

    def x_copy(part, k):
        peer = inner ^ k
        return remote(
            x_ref.at[:, columns(part, peer)],
            x_out.at[inner, :, pl.ds(part * width, width)],
            s_cube.at[2 + part, k], r_cube.at[2 + part, k],
            group, outer * cube + peer,
        )

    for row, (source, rows) in enumerate(((rest_source, rest_rows), (down_source, down_rows))):

        def spread(step, carry, row=row, source=source):
            k = cube - 1 - step
            read_piece(row, k).wait()
            source[k] = dense(row, k)
            cube_copy(row, k).start()
            return carry

        lax.fori_loop(0, cube - 1, spread, 0)
        read_piece(row, 0).wait()
        rows[inner] = dense(row, 0)

    to_table = [pltpu.make_async_copy(stretch_ref, table.at[0], s_table.at[0])]
    to_table[0].start()
    for step, copy in zip(range(1, groups), row_copies):
        copy.wait_recv()
        move = pltpu.make_async_copy(stretch_land.at[step], table.at[step], s_table.at[step])
        move.start()
        to_table.append(move)
    for move in to_table:
        move.wait()

    def slot_of(k):
        return owner_ref[table[k // cubes, 0, outer ^ (k % cubes)]]

    def chosen(part):
        return (part * cubes + lax.div(slot_of(0), cube)) ^ home

    owns = []
    for part in range(groups):
        own = pltpu.make_async_copy(
            x_ref.at[:, columns(part, inner)],
            x_out.at[inner, :, pl.ds(part * width, width)],
            s_own.at[part],
        )
        own.start()
        owns.append(own)

    far = []
    for row, (rows, outgoing, landing) in enumerate(
        ((rest_rows, rest_send, rest_land), (down_rows, down_send, down_land))
    ):
        for k in range(1, cube):
            cube_copy(row, k).wait_recv()
        coming = []
        for k in range(1, kinds):
            there = home ^ k
            outgoing[k] = rows[lax.rem(slot_of(k), cube)]
            copy = remote(
                outgoing.at[k], landing.at[k], s_far.at[row, k], r_far.at[row, k],
                there // cubes, (there % cubes) * cube + inner,
            )
            copy.start()
            coming.append(copy)
        landing[0] = rows[lax.rem(slot_of(0), cube)]
        far.append(coming)

    for copy in far[0]:
        copy.wait_recv()
    for part in range(groups):
        rest_out[part, inner] = rest_land[chosen(part)]
    tree = {}
    have = [[0] for _ in range(groups)]
    levels = cube.bit_length() - 1
    orders = []
    for part in range(groups):
        order = [1 << level for level in reversed(range(levels))]
        if part % 2:
            order[:2] = order[1::-1]
        orders.append(order)
    for stage in range(levels):
        for part in range(groups):
            bit = orders[part][stage]
            before = orders[part][stage - 1] if stage else 0
            for k in have[part]:
                if k & before:
                    tree[k, part].wait_recv()
            new = []
            for k in have[part]:
                slot = rest_out.at[part, inner ^ k]
                copy = remote(
                    slot, slot, s_tree.at[part, k ^ bit], r_tree.at[part, k ^ bit],
                    group, outer * cube + (inner ^ bit),
                )
                copy.start()
                tree[k ^ bit, part] = copy
                new.append(k ^ bit)
            have[part] = have[part] + new
        if stage == 0:
            for part in range(groups):
                for k in reversed(range(1, cube)):
                    x_copy(part, k).start()

    for copy in far[1]:
        copy.wait_recv()
    for part in range(groups):
        down_out[part] = down_land[chosen(part)]
    for (k, part), copy in tree.items():
        if k & orders[part][-1]:
            copy.wait_recv()
    for own in owns:
        own.wait()
    for part in range(groups):
        for k in range(1, cube):
            x_copy(part, k).wait_recv()
            x_copy(part, k).wait_send()
    for row in range(2):
        for k in range(1, cube):
            cube_copy(row, k).wait_send()
    for copy in row_copies + far[0] + far[1] + list(tree.values()):
        copy.wait_send()


def place_adapter(groups, cubes, cube, down_size, owner, stretch_row, x, pool):
    kinds = groups * cubes
    tokens, depth = x.shape
    down_piece = down_size // (groups * cube)
    rest_piece = (pool.shape[1] - down_size) // (groups * cube)
    down_shape = (down_piece // LANES, LANES)
    rest_shape = (rest_piece // LANES, LANES)
    bf16 = jnp.bfloat16
    dma = pltpu.SemaphoreType.DMA
    return pl.pallas_call(
        partial(place_adapter_kernel, groups, cubes, cube, down_size),
        out_shape=(
            jax.ShapeDtypeStruct((cube, tokens, depth // cube), bf16),
            jax.ShapeDtypeStruct((groups,) + down_shape, bf16),
            jax.ShapeDtypeStruct((groups, cube) + rest_shape, bf16),
        ),
        in_specs=[SCALARS, ON_CHIP, ON_CHIP, pl.BlockSpec(memory_space=pl.ANY)],
        out_specs=(ON_CHIP, ON_CHIP, ON_CHIP),
        scratch_shapes=[
            pltpu.VMEM((cube, 1, down_piece), bf16),
            pltpu.VMEM((cube, 1, rest_piece), bf16),
            pltpu.VMEM((cube,) + down_shape, bf16),
            pltpu.VMEM((cube,) + rest_shape, bf16),
            pltpu.VMEM((cube,) + down_shape, bf16),
            pltpu.VMEM((cube,) + rest_shape, bf16),
            pltpu.VMEM((kinds,) + down_shape, bf16),
            pltpu.VMEM((kinds,) + rest_shape, bf16),
            pltpu.VMEM((kinds,) + down_shape, bf16),
            pltpu.VMEM((kinds,) + rest_shape, bf16),
            pltpu.VMEM((groups,) + stretch_row.shape, jnp.int32),
            pltpu.SMEM((groups,) + stretch_row.shape, jnp.int32),
            dma((2, cube)),
            dma((2 + groups, cube)),
            dma((2 + groups, cube)),
            dma((2, kinds)),
            dma((2, kinds)),
            dma((groups, cube)),
            dma((groups, cube)),
            dma((groups,)),
            dma((groups,)),
            dma((groups,)),
            dma((groups,)),
        ],
        compiler_params=pltpu.CompilerParams(
            collective_id=0,
            has_side_effects=True,
            vmem_limit_bytes=22 * 1024 * 1024 + 4 * kinds * (down_piece + rest_piece),
        ),
    )(owner, stretch_row, x, pool)


def keyval_kernel(
    cube, count,
    x_any, w_ref, rest_any, query_ref, key_ref, value_ref, cos_ref, sin_ref,
    query_out, out_ref,
    x_ref, up_ref, s_in, wide, total, outgoing, landing, s_sem, r_sem, s_all, r_all,
):
    group = lax.axis_index("groups")
    ctx = lax.axis_index("ctx")
    inner = ctx % cube
    outer = ctx // cube
    levels = count.bit_length() - 1
    x_in = pltpu.make_async_copy(x_any, x_ref, s_in.at[0])
    x_in.start()
    up_in = pltpu.make_async_copy(
        rest_any.at[pl.ds(0, up_ref.shape[0])], up_ref, s_in.at[1]
    )
    up_in.start()
    barrier = pltpu.get_barrier_semaphore()
    apart = list(range(1, cube)) + [1 << n for n in range(levels) if 1 << n >= cube]
    for k in apart:
        pl.semaphore_signal(barrier, inc=1, device_id=(group, ctx ^ k), device_id_type=MESH)
    _, tokens, depth = x_ref.shape
    x_in.wait()
    product = jnp.dot(
        x_ref[...].reshape(cube * tokens, depth), w_ref[...], preferred_element_type=jnp.float32
    ).reshape(cube, tokens, w_ref.shape[1])
    total[...] = product
    outgoing[...] = product.astype(jnp.bfloat16)
    pl.semaphore_wait(barrier, len(apart))
    copies = []
    for k in range(1, cube):
        peer = inner ^ k
        copy = remote(
            outgoing.at[peer], landing.at[k], s_sem.at[k], r_sem.at[k], group, outer * cube + peer
        )
        copy.start()
        copies.append(copy)
    up_in.wait()
    wide[...] = up_ref[...].astype(jnp.float32)
    result = total[inner]
    for k, copy in zip(range(1, cube), copies):
        copy.wait_recv()
        result = result + landing[k].astype(jnp.float32)
    low = result.astype(jnp.bfloat16)
    half = HEAD_SIZE // 2
    query_rows = ADAPTER_RANK * QH
    kinds = 2 * KEYVALUE_HEADS
    for j in range(2 * KEYVALUE_HEADS):
        first = ADAPTER_RANK * (1 if j < KEYVALUE_HEADS else 2)
        delta = adapter_scale * jnp.dot(
            low[:, first : first + ADAPTER_RANK],
            wide[pl.ds(query_rows + j, ADAPTER_RANK, stride=kinds), :].astype(jnp.bfloat16),
            preferred_element_type=jnp.float32
        )
        base_ref = key_ref if j < KEYVALUE_HEADS else value_ref
        head = j % KEYVALUE_HEADS
        if j < KEYVALUE_HEADS:
            swapped = jnp.concatenate([delta[:, half:], delta[:, :half]], axis=1)
            delta = delta * cos_ref[...] + swapped * sin_ref[...]
        base = base_ref[:, head * HEAD_SIZE : (head + 1) * HEAD_SIZE].astype(jnp.float32)
        out_ref[ctx, :, j * HEAD_SIZE : (j + 1) * HEAD_SIZE] = (base + delta).astype(jnp.bfloat16)

    def query_head(head):
        up = wide[pl.ds(head, ADAPTER_RANK, stride=QH), :].astype(jnp.bfloat16)
        delta = adapter_scale * jnp.dot(
            low[:, :ADAPTER_RANK], up, preferred_element_type=jnp.float32
        )
        swapped = jnp.concatenate([delta[:, half:], delta[:, :half]], axis=1)
        delta = delta * cos_ref[...] + swapped * sin_ref[...]
        base = query_ref[:, head * HEAD_SIZE : (head + 1) * HEAD_SIZE].astype(jnp.float32)
        shared = QH // KEYVALUE_HEADS
        query_out[
            head // shared, (head % shared) * tokens : (head % shared + 1) * tokens, :
        ] = (base + delta).astype(jnp.bfloat16)

    kv_width = KEYVALUE_HEADS * HEAD_SIZE
    far_first = [1 << level for level in reversed(range(levels))]
    orders = (far_first, [2] + [bit for bit in far_first if bit != 2])
    have = [[0], [0]]
    moved = {}
    done = 0
    for stage in range(levels):
        for part in range(2):
            bit = orders[part][stage]
            before = orders[part][stage - 1] if stage else 0
            new = []
            for k in have[part]:
                if k & before:
                    moved[k, part].wait_recv()
                slot = out_ref.at[ctx ^ k, :, pl.ds(part * kv_width, kv_width)]
                copy = remote(
                    slot, slot, s_all.at[part, k ^ bit], r_all.at[part, k ^ bit], group, ctx ^ bit
                )
                copy.start()
                moved[k ^ bit, part] = copy
                new.append(k ^ bit)
            have[part] = have[part] + new
        until = QH * (stage + 1) // levels
        for head in range(done, until):
            query_head(head)
        done = until
    for (k, part), copy in moved.items():
        if k & orders[part][-1]:
            copy.wait_recv()
    for copy in copies + list(moved.values()):
        copy.wait_send()


def keyval(cube, count, x, w, rest, query_rows, key_rows, value_rows, cosine, sine):
    _, tokens, _ = x.shape
    shape = (cube, tokens, w.shape[1])
    up_rows = ADAPTER_RANK * (QH + 2 * KEYVALUE_HEADS)
    dma = pltpu.SemaphoreType.DMA
    return pl.pallas_call(
        partial(keyval_kernel, cube, count),
        out_shape=(
            jax.ShapeDtypeStruct(
                (KEYVALUE_HEADS, QH // KEYVALUE_HEADS * tokens, HEAD_SIZE), jnp.bfloat16
            ),
            jax.ShapeDtypeStruct(
                (count, tokens, 2 * KEYVALUE_HEADS * HEAD_SIZE), jnp.bfloat16
            ),
        ),
        in_specs=[ANYWHERE, ON_CHIP, ANYWHERE] + [ON_CHIP] * 5,
        out_specs=(ON_CHIP, ON_CHIP),
        scratch_shapes=[
            pltpu.VMEM(x.shape, jnp.bfloat16),
            pltpu.VMEM((up_rows, LANES), jnp.bfloat16),
            dma((2,)),
            pltpu.VMEM((up_rows, LANES), jnp.float32),
            pltpu.VMEM(shape, jnp.float32),
            pltpu.VMEM(shape, jnp.bfloat16),
            pltpu.VMEM(shape, jnp.bfloat16),
            dma((cube,)),
            dma((cube,)),
            dma((2, count)),
            dma((2, count)),
        ],
        compiler_params=pltpu.CompilerParams(
            collective_id=1,
            has_side_effects=True,
            vmem_limit_bytes=16 * 1024 * 1024
            + 4 * count * tokens * KEYVALUE_HEADS * HEAD_SIZE,
        ),
    )(x, w, rest, query_rows, key_rows, value_rows, cosine, sine)


def attend_kernel(
    step_keys, queries, kv_ref, rest_any,
    attended_ref, delta_ref,
    rest_ref, s_in, wide, permuted, run_max, run_sum, run_acc,
):
    tokens = attended_ref.shape[0]
    ctx = lax.axis_index("ctx")
    heads = QH // KEYVALUE_HEADS
    rows = heads * tokens
    half = HEAD_SIZE // 2
    query_rows = ADAPTER_RANK * QH
    raise_start = QH * half
    rest_in = pltpu.make_async_copy(
        rest_any.at[pl.ds(query_rows + 2 * ADAPTER_RANK * KEYVALUE_HEADS, rest_ref.shape[0])],
        rest_ref,
        s_in,
    )
    rest_in.start()
    first = ctx * tokens
    steps = (first + tokens + step_keys - 1) // step_keys
    row = lax.broadcasted_iota(jnp.int32, (rows, step_keys), 0)
    query_pos = first + lax.rem(row, tokens)
    key_off = lax.broadcasted_iota(jnp.int32, (rows, step_keys), 1)
    source = lax.broadcasted_iota(jnp.int32, (HEAD_SIZE, HEAD_SIZE), 0)
    target = lax.broadcasted_iota(jnp.int32, (HEAD_SIZE, HEAD_SIZE), 1)
    wanted = jnp.where(target < half, 2 * target, 2 * (target - half) + 1)
    shuffle = jnp.where(source == wanted, 1.0, 0.0).astype(jnp.bfloat16)
    for group in range(KEYVALUE_HEADS):
        run_max[...] = jnp.full_like(run_max, mask_floor)
        run_sum[...] = jnp.zeros_like(run_sum)
        run_acc[...] = jnp.zeros_like(run_acc)
        key_cols = slice(group * HEAD_SIZE, (group + 1) * HEAD_SIZE)
        value_first = (KEYVALUE_HEADS + group) * HEAD_SIZE

        def advance(step, carry):
            start = pl.multiple_of(step * step_keys, step_keys)
            keys = kv_ref[pl.ds(start, step_keys), key_cols]
            values = kv_ref[pl.ds(start, step_keys), value_first : value_first + HEAD_SIZE]
            scores = lax.dot_general(
                queries[group], keys, (((1,), (1,)), ((), ())),
                preferred_element_type=jnp.float32,
            ) * HEAD_SIZE ** (-0.5)
            scores = jnp.where(query_pos >= key_off + start, scores, mask_floor)
            new_max = jnp.maximum(run_max[...], jnp.max(scores, axis=1, keepdims=True))
            weights = jnp.exp(scores - new_max)
            rescale = jnp.exp(run_max[...] - new_max)
            run_sum[...] = run_sum[...] * rescale + jnp.sum(weights, axis=1, keepdims=True)
            run_acc[...] = run_acc[...] * rescale + jnp.dot(
                weights.astype(jnp.bfloat16), values, preferred_element_type=jnp.float32
            )
            run_max[...] = new_max
            return carry

        lax.fori_loop(0, steps, advance, 0)
        result = (run_acc[...] / run_sum[...]).astype(jnp.bfloat16)
        mixed = jnp.dot(result, shuffle, preferred_element_type=jnp.float32).astype(jnp.bfloat16)
        for j in range(heads):
            head = group * heads + j
            cols = slice(head * HEAD_SIZE, (head + 1) * HEAD_SIZE)
            attended_ref[:, cols] = result[j * tokens : (j + 1) * tokens]
            permuted[:, cols] = mixed[j * tokens : (j + 1) * tokens]
    rest_in.wait()
    wide[...] = rest_ref[raise_start:, :].astype(jnp.float32)
    narrow = jnp.zeros((tokens, ADAPTER_RANK), jnp.float32)
    for head in range(QH):
        block = rest_ref[head * half : (head + 1) * half, :]
        weight = jnp.concatenate([block[:, :half], block[:, half:]], axis=0)
        narrow = narrow + jnp.dot(
            permuted[:, head * HEAD_SIZE : (head + 1) * HEAD_SIZE],
            weight,
            preferred_element_type=jnp.float32,
        )
    narrow = narrow.astype(jnp.bfloat16)
    blocks = D // LANES
    for j in range(blocks):
        up = wide[pl.ds(j, ADAPTER_RANK, stride=blocks), :].astype(jnp.bfloat16)
        delta_ref[:, j * LANES : (j + 1) * LANES] = (
            adapter_scale * jnp.dot(narrow, up, preferred_element_type=jnp.float32)
        ).astype(jnp.bfloat16)


def attend(queries, kv, rest):
    rows = queries.shape[1]
    tokens = rows // (QH // KEYVALUE_HEADS)
    out_rows = ADAPTER_RANK * (QH * HEAD_SIZE + D) // LANES
    return pl.pallas_call(
        partial(attend_kernel, math.gcd(kv.shape[0], 1024)),
        out_shape=(
            jax.ShapeDtypeStruct((tokens, QH * HEAD_SIZE), jnp.bfloat16),
            jax.ShapeDtypeStruct((tokens, D), jnp.bfloat16),
        ),
        in_specs=[ON_CHIP, ON_CHIP, ANYWHERE],
        out_specs=(ON_CHIP, ON_CHIP),
        scratch_shapes=[
            pltpu.VMEM((out_rows, LANES), jnp.bfloat16),
            pltpu.SemaphoreType.DMA,
            pltpu.VMEM((ADAPTER_RANK * D // LANES, LANES), jnp.float32),
            pltpu.VMEM((tokens, QH * HEAD_SIZE), jnp.bfloat16),
            pltpu.VMEM((rows, 1), jnp.float32),
            pltpu.VMEM((rows, 1), jnp.float32),
            pltpu.VMEM((rows, HEAD_SIZE), jnp.float32),
        ],
        compiler_params=pltpu.CompilerParams(vmem_limit_bytes=56 * 1024 * 1024),
    )(queries, kv, rest)


def shards(
    normed_input, query_base, key_base, value_base, adapter_pool, stretch_adapter, adapter_owner
):
    cycle_size = lax.axis_size("ctx")
    my_index = lax.axis_index("ctx")
    tok_rows = normed_input.shape[0]
    token_positions = my_index * tok_rows + jnp.arange(tok_rows, dtype=jnp.int32)
    groups = lax.axis_size("groups")
    cube = BLOCK_TOKENS // tok_rows
    cubes = cycle_size // cube
    padding = -stretch_adapter.shape[0] % LANES
    stretch_row = jnp.pad(stretch_adapter, (0, padding))[None]
    down_size = 3 * ADAPTER_RANK * D
    half_dim = HEAD_SIZE // 2
    frequency = rope_base ** (-(jnp.arange(half_dim, dtype=jnp.float32) * 2.0) / HEAD_SIZE)
    angle = token_positions.astype(jnp.float32)[:, None] * frequency[None, :]
    cosine = jnp.cos(angle)
    sine = jnp.sin(angle)
    cosine = jnp.concatenate([cosine, cosine], axis=1)
    sine = jnp.concatenate([-sine, sine], axis=1)
    moved, down_slice, rest = place_adapter(
        groups, cubes, cube, down_size, adapter_owner, stretch_row, normed_input, adapter_pool
    )
    rest = rest.reshape(-1, LANES)
    queries, gathered = keyval(
        cube,
        cycle_size,
        moved,
        down_slice.reshape(D // cube, 3 * ADAPTER_RANK),
        rest,
        query_base,
        key_base,
        value_base,
        cosine,
        sine,
    )
    gathered = gathered.reshape(cycle_size * tok_rows, -1)
    return attend(queries, gathered, rest)


def solution(mesh):
    placed = (
        P(("groups", "ctx"), None),
        P(("groups", "ctx"), None),
        P(("groups", "ctx"), None),
        P(("groups", "ctx"), None),
        P("ctx", None),
        P("groups"),
        P(),
    )
    return jax.shard_map(
        shards,
        mesh=mesh,
        in_specs=placed,
        out_specs=(P(("groups", "ctx"), None), P(("groups", "ctx"), None)),
        check_vma=False,
    )
```
